256 devices in a mesh: sec: 4 (over x), px: 16 (over z, core), py: 4 (over y).
Axes of the slice: x: 4, y: 4, z: 8, core: 2. Of those that a mesh axis runs over, the one named last changes fastest.
Arguments:
- background: bfloat16 [2, 4, 512, 8192], P(None, 'sec', 'px', 'py'), may hold values from -6 to 6
- src_pos: int32 [16], replicated, may hold values from 0 to 1048575
- coupling: bfloat16 [4, 512, 512], P('sec', 'px'), may hold values from 0.3984375 to 1
- x_factor: bfloat16 [4, 2, 512, 512], P('sec', None, ('px', 'py')), may hold values from -1.25 to 1.25, as said below
- y_factor: bfloat16 [4, 2, 512, 512], P('sec', None, ('px', 'py')), may hold values from -1.25 to 1.25, as said below
Outputs:
- sweep_out: bfloat16 [2, 4, 512, 8192], P(None, 'sec', 'px', 'py')
The draws below stay inside these ranges and needn't reach their ends.
Inputs may be any that keep to these rules, and one draw needn't show every extreme that they name: `x_factor`: factor entries; each is a dense complex matrix. `y_factor`: factor entries; each is a dense complex matrix.
All inputs are finite; a program needn't handle non-finite values.
Results may differ from the reference program's by a relative error of at most 0.02.
Values may be sent and summed in bfloat16 or wider, within the bound.
A program may use at most 64 MiB of HBM per device.

```python
import math
import jax
import jax.numpy as jnp

NX = 512
NY = 512
NSRC = 16
LAYERS = 4


def front_factor(key, layer_count, matrix_order):
    phase_key = jax.random.fold_in(key, 11)
    spread_key = jax.random.fold_in(key, 12)
    phases = jax.random.uniform(phase_key, (layer_count, matrix_order), jnp.float32, -math.pi, math.pi)
    spread = jnp.clip(jax.random.normal(spread_key, (layer_count, 2, matrix_order, matrix_order), jnp.float32), -4.0, 4.0)
    spread = spread * (0.5 / math.sqrt(matrix_order))
    identity = jnp.eye(matrix_order, dtype=jnp.float32)
    diagonal = jnp.stack([jnp.cos(phases), jnp.sin(phases)], axis=1)[:, :, :, None] * identity
    return (spread + diagonal).astype(jnp.bfloat16)


def draw_x_factor(key, part):
    return front_factor(key, LAYERS, NX)


def draw_y_factor(key, part):
    return front_factor(jax.random.fold_in(key, 5), LAYERS, NY)


def place_ends(entries, stream_key, low, high):
    shape = entries.shape
    spot = [jax.random.randint(jax.random.fold_in(stream_key, axis), (), 0, shape[axis]) for axis in range(len(shape))]
    entries = entries.at[tuple(spot)].set(low)
    longest = shape.index(max(shape))
    spot[longest] = (spot[longest] + 1) % shape[longest]
    return entries.at[tuple(spot)].set(high)


def shard_levels(stream_key, dims, shards, least, top_value):
    def one(axis_at, blocks):
        draws = jax.random.uniform(jax.random.fold_in(jax.random.fold_in(stream_key, 6), axis_at), (blocks,), jnp.float32, least / len(shards), top_value / len(shards))
        return jnp.repeat(jnp.exp(draws), dims[axis_at] // blocks).reshape((-1,) + (1,) * (len(dims) - axis_at - 1))

    factor_of = one(*shards[0])
    for cut in shards[1:]:
        factor_of = factor_of * one(*cut)
    return factor_of


def bell_draw(stream_key, extent, scale, limit, pieces=(), kind=jnp.bfloat16):
    factor_of = shard_levels(stream_key, extent, pieces, -0.22, 0.18) if pieces else 1.0
    entries = jax.random.normal(stream_key, extent, jnp.float32) * scale * factor_of
    return jnp.minimum(jnp.maximum(entries, -limit), limit).astype(kind)


def setup_inputs(seed: int = 0) -> dict:
    streams_of = jax.random.split(jax.random.key(seed), 6)
    return {
        "background": bell_draw(streams_of[0], (2, LAYERS, NX, NSRC * NY), 1.0, 6.0, ((1, 4), (2, 16), (3, 4))),
        "src_pos": place_ends(jax.random.randint(streams_of[1], (NSRC,), 0, LAYERS * NX * NY), jax.random.fold_in(streams_of[1], 1), 0, (LAYERS * NX * NY) - 1).astype(jnp.int32),
        "coupling": jnp.clip(0.3984375 + 0.6015625 * jax.random.uniform(streams_of[2], (LAYERS, NX, NY), jnp.float32) ** shard_levels(streams_of[2], (LAYERS, NX, NY), ((0, 4), (1, 16)), -0.2, 0.2), 0.3984375, 1.0).astype(jnp.bfloat16),
        "x_factor": draw_x_factor(jax.random.fold_in(streams_of[5], 71), 0),
        "y_factor": draw_y_factor(jax.random.fold_in(streams_of[5], 71), 0),
    }


source_amplitude = 8.0


def transform(factor, field_in, pattern):
    factor32 = factor.astype(jnp.float32)
    field32 = field_in.astype(jnp.float32)
    real_part = jnp.einsum(pattern, factor32[0], field32[0]) - jnp.einsum(pattern, factor32[1], field32[1])
    imag_part = jnp.einsum(pattern, factor32[0], field32[1]) + jnp.einsum(pattern, factor32[1], field32[0])
    return jnp.stack([real_part, imag_part]).astype(jnp.bfloat16)


def apply_front(x_layer, y_layer, field_in):
    inner_field = transform(y_layer, field_in, "yk,xsk->xsy")
    return transform(x_layer, inner_field, "xk,ksy->xsy")


def reference(background, src_pos, coupling, x_factor, y_factor):
    rhs_field = background.astype(jnp.float32).reshape(2, LAYERS, NX, NSRC, NY)
    layer_of = src_pos // (NX * NY)
    remainder = src_pos % (NX * NY)
    row_of = remainder // NY
    column_of = remainder % NY
    sources = jnp.arange(NSRC, dtype=jnp.int32)
    rhs_field = rhs_field.at[0, layer_of, row_of, sources, column_of].add(source_amplitude)
    weights = coupling.astype(jnp.float32)[:, None, :, None, :]
    forward = []
    previous = jnp.zeros((2, NX, NSRC, NY), jnp.bfloat16)
    for layer_index in range(LAYERS):
        reduced = (rhs_field[:, layer_index] - weights[layer_index] * previous.astype(jnp.float32)).astype(jnp.bfloat16)
        previous = apply_front(x_factor[layer_index], y_factor[layer_index], reduced)
        forward.append(previous)
    result = [forward[LAYERS - 1] for layer_index in range(LAYERS)]
    later_field = forward[LAYERS - 1]
    for layer_index in range(LAYERS - 2, -1, -1):
        sent_field = (weights[layer_index + 1] * later_field.astype(jnp.float32)).astype(jnp.bfloat16)
        solved = apply_front(x_factor[layer_index], y_factor[layer_index], sent_field)
        later_field = (forward[layer_index].astype(jnp.float32) - solved.astype(jnp.float32)).astype(jnp.bfloat16)
        result[layer_index] = later_field
    return jnp.stack(result, axis=1).reshape(2, LAYERS, NX, NSRC * NY)
```

```python
import jax
import jax.numpy as jnp
from jax import lax
from jax.experimental import pallas as pl
from jax.experimental.pallas import tpu as pltpu
from jax.sharding import PartitionSpec as P

MESH = pl.DeviceIdType.MESH
source_amplitude = 8.0
f32 = jnp.float32
bf16 = jnp.bfloat16


def consumer_z(q, j, chips):
    return lax.rem(2 * q + j, chips)


def sweep_kernel(
    dims, src_ref, bg_ref, cp_ref, xf_ref, yf_ref, out_ref,
    landing, relay, factor, field, weights, sent, turned,
    send_sem, direct_sem, relay_sem, via_sem, field_sem, weight_sem, out_send, out_sem,
):
    secs, columns, grid_y, size = dims
    chips = columns // 2
    rows = size // columns
    q = lax.axis_index("sec")
    p = lax.axis_index("px")
    j = lax.axis_index("py")
    block = p * grid_y + j
    consumers = secs * grid_y
    devices = secs * columns * grid_y

    my_z = consumer_z(q, j, chips)
    is_consumer = p == 2 * my_z
    up_z = lax.rem(my_z + 1, chips)
    down_z = lax.rem(my_z + chips - 1, chips)
    is_up = p == 2 * up_z + 1
    is_down = p == 2 * down_z + 1
    is_relay = is_up | is_down

    barrier = pltpu.get_barrier_semaphore()

    @pl.when(is_consumer | is_relay)
    def _():
        def tell(i, carry):
            a = i // (columns * grid_y)
            r = lax.rem(i, columns * grid_y)
            pl.semaphore_signal(
                barrier, inc=1, device_id=(a, r // grid_y, lax.rem(r, grid_y)), device_id_type=MESH
            )
            return carry

        lax.fori_loop(0, devices, tell, 0)

    def announce(a, carry):
        pl.semaphore_signal(
            barrier, inc=1, device_id=(a, 2 * consumer_z(a, j, chips), j), device_id_type=MESH
        )
        return carry

    lax.fori_loop(0, secs, announce, 0)

    @pl.when(is_consumer)
    def _():
        pl.semaphore_wait(barrier, 3 * consumers + secs * columns)

    @pl.when(jnp.logical_not(is_consumer))
    def _():
        pl.semaphore_wait(barrier, 3 * consumers)

    def push(src, dst, recv, device, is_self):
        @pl.when(is_self)
        def _():
            pltpu.make_async_copy(src, dst, recv).start()

        @pl.when(jnp.logical_not(is_self))
        def _():
            pltpu.make_async_remote_copy(
                src_ref=src, dst_ref=dst, send_sem=send_sem, recv_sem=recv,
                device_id=device, device_id_type=MESH,
            ).start()

    def spread(i, carry):
        a = i // grid_y
        b = lax.rem(i, grid_y)
        z = consumer_z(a, b, chips)
        here = (a == q) & (b == j)
        push(
            yf_ref.at[0], landing.at[q, pl.ds(2, 2), block], direct_sem.at[q],
            (a, 2 * z, b), here & is_consumer,
        )
        push(
            xf_ref.at[0, 0], relay.at[q, block], relay_sem.at[q],
            (a, 2 * lax.rem(z + 1, chips) + 1, b), here & is_up,
        )
        push(
            xf_ref.at[0, 1], relay.at[q, block], relay_sem.at[q],
            (a, 2 * lax.rem(z + chips - 1, chips) + 1, b), here & is_down,
        )
        return carry

    lax.fori_loop(0, consumers, spread, 0)
    for a in range(secs):
        z = consumer_z(a, j, chips)
        own = pl.ds(pl.multiple_of(p * rows, rows), rows)
        here = (a == q) & is_consumer
        push(
            bg_ref.at[:, 0, :, pl.ds(a * size, size)], field.at[q, :, own, :], field_sem.at[q],
            (a, 2 * z, j), here,
        )
        push(cp_ref.at[0], weights.at[q, own, :], weight_sem.at[q], (a, 2 * z, j), here)

    def await_bytes(ref, sem):
        pltpu.make_async_copy(ref, ref, sem).wait()

    @pl.when(is_relay)
    def _():
        part = jnp.where(is_up, 0, 1)

        def forward(layer, carry):
            await_bytes(relay.at[layer], relay_sem.at[layer])
            pltpu.make_async_remote_copy(
                src_ref=relay.at[layer], dst_ref=landing.at[layer, part], send_sem=out_send,
                recv_sem=via_sem.at[part, layer], device_id=(q, 2 * my_z, j), device_id_type=MESH,
            ).start()
            return carry

        lax.fori_loop(0, secs, forward, 0)
        await_bytes(relay, out_send)

    @pl.when(is_consumer)
    def _():
        position = src_ref[j * secs + q]
        layer_of = position // (size * size)
        inside = position - layer_of * (size * size)
        row_of = inside // size
        column_of = inside - row_of * size
        row_ids = lax.broadcasted_iota(jnp.int32, (size, 1), 0)
        column_ids = lax.broadcasted_iota(jnp.int32, (1, size), 1)

        def dot(a, b):
            return jnp.dot(a, b, preferred_element_type=f32)

        def dot_turned(a, b):
            return lax.dot_general(a, b, (((1,), (1,)), ((), ())), preferred_element_type=f32)

        def front(layer, source):
            vr = source[0]
            vi = source[1]
            yr = factor[layer, 2]
            yi = factor[layer, 3]
            turned[0] = (dot_turned(vr, yr) - dot_turned(vi, yi)).astype(bf16)
            turned[1] = (dot_turned(vr, yi) + dot_turned(vi, yr)).astype(bf16)
            xr = factor[layer, 0]
            xi = factor[layer, 1]
            real = dot(xr, turned[0]) - dot(xi, turned[1])
            yield 0, real
            yield 1, dot(xr, turned[1]) + dot(xi, turned[0])

        def gather_rows(layer, planes):
            def step(k, carry):
                for m in planes:
                    tile = jnp.concatenate([landing[layer, m, 4 * k + i] for i in range(4)], axis=0)
                    factor[layer, m, pl.ds(pl.multiple_of(k * 32, 32), 32), :] = tile
                return carry

            lax.fori_loop(0, size // 32, step, 0)

        def emit(layer):
            def one(k, carry):
                piece = field.at[layer, :, pl.ds(pl.multiple_of(k * rows, rows), rows), :]
                target = out_ref.at[:, 0, :, pl.ds(pl.multiple_of(q * size, size), size)]
                here = (layer == q) & (k == p)

                @pl.when(here)
                def _():
                    pltpu.make_async_copy(piece, target, out_sem).start()

                @pl.when(jnp.logical_not(here))
                def _():
                    pltpu.make_async_remote_copy(
                        src_ref=piece, dst_ref=target, send_sem=out_send, recv_sem=out_sem,
                        device_id=(layer, k, j), device_id_type=MESH,
                    ).start()

                return carry

            lax.fori_loop(0, columns, one, 0)

        def forward(layer, carry):
            await_bytes(field.at[layer], field_sem.at[layer])
            await_bytes(weights.at[layer], weight_sem.at[layer])
            strength = jnp.where(layer_of == layer, source_amplitude, 0.0).astype(f32)
            bump = jnp.where(row_ids == row_of, strength, 0.0) * jnp.where(
                column_ids == column_of, 1.0, 0.0
            )

            @pl.when(layer == 0)
            def _():
                sent[0] = (field[0, 0].astype(f32) + bump).astype(bf16)
                sent[1] = field[0, 1]

            @pl.when(layer > 0)
            def _():
                scale = weights[layer].astype(f32)
                before = jnp.maximum(layer - 1, 0)
                sent[0] = (
                    field[layer, 0].astype(f32) + bump - scale * field[before, 0].astype(f32)
                ).astype(bf16)
                sent[1] = (
                    field[layer, 1].astype(f32) - scale * field[before, 1].astype(f32)
                ).astype(bf16)

            await_bytes(landing.at[layer, pl.ds(2, 2)], direct_sem.at[layer])
            gather_rows(layer, (2, 3))
            await_bytes(landing.at[layer, 0], via_sem.at[0, layer])
            await_bytes(landing.at[layer, 1], via_sem.at[1, layer])
            gather_rows(layer, (0, 1))
            for plane, value in front(layer, sent):
                field[layer, plane] = value.astype(bf16)
            return carry

        lax.fori_loop(0, secs, forward, 0)
        emit(secs - 1)

        def backward(step, carry):
            layer = secs - 2 - step
            scale = weights[layer + 1].astype(f32)
            sent[0] = (scale * field[layer + 1, 0].astype(f32)).astype(bf16)
            sent[1] = (scale * field[layer + 1, 1].astype(f32)).astype(bf16)
            for plane, value in front(layer, sent):
                solved = value.astype(bf16).astype(f32)
                field[layer, plane] = (field[layer, plane].astype(f32) - solved).astype(bf16)
            emit(layer)
            return carry

        lax.fori_loop(0, secs - 1, backward, 0)
        await_bytes(field.at[pl.ds(0, secs - 1)], out_send)
        await_bytes(field.at[0, :, pl.ds(0, size - rows), :], out_send)

    def sent_out(factor_bytes, field_blocks):
        pass

    await_bytes(landing.at[0, 0, pl.ds(0, 60)], send_sem)

    @pl.when(is_consumer)
    def _():
        await_bytes(landing.at[0, 0, pl.ds(0, 2)], send_sem)
        await_bytes(field.at[0, :, pl.ds(0, rows * (secs - 1)), :], send_sem)
        await_bytes(weights.at[0, pl.ds(0, rows * (secs - 1)), :], send_sem)

    @pl.when(is_relay)
    def _():
        await_bytes(landing.at[0, 0, pl.ds(0, 3)], send_sem)

    @pl.when(jnp.logical_not(is_relay | is_consumer))
    def _():
        await_bytes(landing.at[0, 0, pl.ds(0, 4)], send_sem)

    @pl.when(jnp.logical_not(is_consumer))
    def _():
        await_bytes(field.at[0, :, pl.ds(0, rows * secs), :], send_sem)
        await_bytes(weights.at[0, pl.ds(0, rows * secs), :], send_sem)

    await_bytes(out_ref, out_sem)


def solution(mesh):
    secs = mesh.shape["sec"]
    columns = mesh.shape["px"]
    grid_y = mesh.shape["py"]

    def on_device(background, src_pos, coupling, x_factor, y_factor):
        size = x_factor.shape[3]
        blocks = columns * grid_y
        height = x_factor.shape[2]
        dims = (secs, columns, grid_y, size)

        def body(*refs):
            sweep_kernel(dims, *refs)

        any_spec = pl.BlockSpec(memory_space=pl.ANY)
        dma = pltpu.SemaphoreType.DMA
        return pl.pallas_call(
            body,
            out_shape=jax.ShapeDtypeStruct(background.shape, bf16),
            in_specs=[pl.BlockSpec(memory_space=pltpu.SMEM)] + [any_spec] * 4,
            out_specs=any_spec,
            scratch_shapes=[
                pltpu.VMEM((secs, 4, blocks, height, size), bf16),
                pltpu.VMEM((secs, blocks, height, size), bf16),
                pltpu.VMEM((secs, 4, size, size), bf16),
                pltpu.VMEM((secs, 2, size, size), bf16),
                pltpu.VMEM((secs, size, size), bf16),
                pltpu.VMEM((2, size, size), bf16),
                pltpu.VMEM((2, size, size), bf16),
                dma, dma((secs,)), dma((secs,)), dma((2, secs)), dma((secs,)), dma((secs,)),
                dma, dma,
            ],
            compiler_params=pltpu.CompilerParams(
                collective_id=0, has_side_effects=True, vmem_limit_bytes=60 * 2**20
            ),
            name="sweep",
        )(src_pos, background, coupling, x_factor, y_factor)

    placed = (
        P(None, "sec", "px", "py"),
        P(),
        P("sec", "px", None),
        P("sec", None, ("px", "py"), None),
        P("sec", None, ("px", "py"), None),
    )
    return jax.shard_map(
        on_device, mesh=mesh, in_specs=placed, out_specs=P(None, "sec", "px", "py"), check_vma=False
    )
```

```python
import jax
import jax.numpy as jnp
from jax import lax
from jax.experimental import pallas as pl
from jax.experimental.pallas import tpu as pltpu
from jax.sharding import PartitionSpec as P

MESH = pl.DeviceIdType.MESH
source_amplitude = 8.0
f32 = jnp.float32
bf16 = jnp.bfloat16


def sweep_kernel(
    dims, src_ref, bg_ref, cp_ref, xf_ref, yf_ref, out_ref,
    landing, stage, stage_w, factor, field, weights, sent, turned,
    block_send, swap_send, field_send, relay_send, out_send,
    block_sem, swap_sem, swap_w_sem, ring_sem, plane_sem, field_sem, weight_sem, out_sem,
):
    secs, columns, grid_y, size = dims
    rows = size // columns
    q = lax.axis_index("sec")
    p = lax.axis_index("px")
    j = lax.axis_index("py")
    group = p // grid_y
    inner = lax.rem(p, grid_y)
    is_consumer = p == 0
    is_relay = p == 1
    hub = (group, 1, j)
    is_own_hub = is_relay & (q == group)

    barrier = pltpu.get_barrier_semaphore()

    def greet(device):
        pl.semaphore_signal(barrier, inc=1, device_id=device, device_id_type=MESH)

    for step in range(1, secs):
        greet((lax.rem(q + step, secs), p, j))

    @pl.when(is_relay)
    def _():
        def tell(i, carry):
            greet((i // grid_y, q * grid_y + lax.rem(i, grid_y), j))
            return carry

        lax.fori_loop(0, secs * grid_y, tell, 0)
        for step in range(1, secs):
            greet((lax.rem(q + step, secs), 1, j))
        for step in range(1, grid_y):
            greet((q, 1, lax.rem(j + step, grid_y)))

    @pl.when(is_consumer)
    def _():
        def tell(i, carry):
            greet((q, i, j))
            return carry

        lax.fori_loop(0, columns, tell, 0)

    for a in range(secs):
        greet((a, 0, j))

    expected = secs + 1 + jnp.where(is_consumer, secs * columns, 0)
    expected = expected + jnp.where(is_relay, secs + grid_y - 2, 0)
    pl.semaphore_wait(barrier, expected)

    def await_bytes(ref, sem):
        pltpu.make_async_copy(ref, ref, sem).wait()

    def send(src, dst, send_sem, recv_sem, device):
        pltpu.make_async_remote_copy(
            src_ref=src, dst_ref=dst, send_sem=send_sem, recv_sem=recv_sem,
            device_id=device, device_id_type=MESH,
        ).start()

    def push(src, dst, send_sem, recv_sem, device, is_self):
        @pl.when(is_self)
        def _():
            pltpu.make_async_copy(src, dst, recv_sem).start()

        @pl.when(jnp.logical_not(is_self))
        def _():
            send(src, dst, send_sem, recv_sem, device)

    push(
        yf_ref.at[0], landing.at[q, pl.ds(2, 2), group, j, inner], block_send, block_sem.at[q],
        hub, is_own_hub,
    )
    push(
        xf_ref.at[0], landing.at[q, pl.ds(0, 2), group, j, inner], block_send, block_sem.at[q],
        hub, is_own_hub,
    )

    def source_block(a):
        return bg_ref.at[:, 0, :, pl.ds(pl.multiple_of(a * size, size), size)]

    for step in range(1, secs):
        a = lax.rem(q + step, secs)
        send(source_block(a), stage.at[q], swap_send, swap_sem.at[q], (a, p, j))

        @pl.when(q > 0)
        def _():
            send(cp_ref.at[0], stage_w.at[q], swap_send, swap_w_sem.at[q], (a, p, j))

    own = pl.ds(pl.multiple_of(p * rows, rows), rows)
    home = (q, 0, j)
    for layer in range(secs):

        @pl.when(q == layer)
        def _():
            push(
                source_block(q), field.at[layer, :, own, :], field_send, field_sem.at[layer],
                home, is_consumer,
            )
            if layer:
                push(
                    cp_ref.at[0], weights.at[layer, own, :], field_send, weight_sem.at[layer],
                    home, is_consumer,
                )

        @pl.when(q != layer)
        def _():
            await_bytes(stage.at[layer], swap_sem.at[layer])
            push(
                stage.at[layer], field.at[layer, :, own, :], field_send, field_sem.at[layer],
                home, is_consumer,
            )
            if layer:
                await_bytes(stage_w.at[layer], swap_w_sem.at[layer])
                push(
                    stage_w.at[layer], weights.at[layer, own, :], field_send, weight_sem.at[layer],
                    home, is_consumer,
                )

    @pl.when(is_relay)
    def _():
        xs = [lax.rem(q + step, secs) for step in range(secs)]
        ys = [lax.rem(j + step, grid_y) for step in range(grid_y)]
        first = pl.ds(0, 2)
        second = pl.ds(2, 2)

        def open_layer(layer):
            await_bytes(landing.at[layer, :, 0, 0], block_sem.at[layer])
            piece = landing.at[layer, second, q, j]
            for y in ys[1:]:
                send(piece, piece, relay_send, ring_sem.at[0, layer], (q, 1, y))
            piece = landing.at[layer, first, q, j]
            for x in xs[1:]:
                send(piece, piece, relay_send, ring_sem.at[1, layer], (x, 1, j))

        def share(layer):
            await_bytes(landing.at[layer, second, 0, pl.ds(0, grid_y - 1)], ring_sem.at[0, layer])
            piece = landing.at[layer, second, q]
            send(piece, piece, relay_send, ring_sem.at[2, layer], (xs[1], 1, j))
            send(piece, piece, relay_send, ring_sem.at[3, layer], (xs[-1], 1, j))
            await_bytes(landing.at[layer, first, pl.ds(0, secs - 1), 0], ring_sem.at[1, layer])
            piece = landing.at[layer, first, :, j]
            send(piece, piece, relay_send, ring_sem.at[4, layer], (q, 1, ys[1]))
            send(piece, piece, relay_send, ring_sem.at[5, layer], (q, 1, ys[-1]))

        def relay(layer):
            await_bytes(landing.at[layer, second, 0], ring_sem.at[2, layer])
            piece = landing.at[layer, 2, xs[-1]]
            send(piece, piece, relay_send, ring_sem.at[6, layer], (xs[1], 1, j))
            await_bytes(landing.at[layer, second, 0], ring_sem.at[3, layer])
            piece = landing.at[layer, 3, xs[1]]
            send(piece, piece, relay_send, ring_sem.at[7, layer], (xs[-1], 1, j))
            await_bytes(landing.at[layer, first, :, 0], ring_sem.at[4, layer])
            piece = landing.at[layer, 0, :, ys[-1]]
            send(piece, piece, relay_send, ring_sem.at[8, layer], (q, 1, ys[1]))
            await_bytes(landing.at[layer, first, :, 0], ring_sem.at[5, layer])
            piece = landing.at[layer, 1, :, ys[1]]
            send(piece, piece, relay_send, ring_sem.at[9, layer], (q, 1, ys[-1]))

        def close_layer(layer):
            await_bytes(landing.at[layer, 2, 0], ring_sem.at[6, layer])
            await_bytes(landing.at[layer, 3, 0], ring_sem.at[7, layer])
            piece = landing.at[layer, second]
            send(piece, piece, relay_send, plane_sem.at[1, layer], home)
            await_bytes(landing.at[layer, 0, :, 0], ring_sem.at[8, layer])
            await_bytes(landing.at[layer, 1, :, 0], ring_sem.at[9, layer])
            piece = landing.at[layer, first]
            send(piece, piece, relay_send, plane_sem.at[0, layer], home)

        for tick in range(secs + 3):
            if tick == 0:
                for layer in range(secs):
                    open_layer(layer)
            if tick < secs:
                share(tick)
            if 1 <= tick <= secs:
                relay(tick - 1)
            if 2 <= tick <= secs + 1:
                close_layer(tick - 2)
        for layer in range(secs):
            for step in range(1, secs):
                await_bytes(landing.at[layer, second, 0, 0], relay_send)
                await_bytes(landing.at[layer, first, 0, 0], relay_send)
            for side in range(2):
                await_bytes(landing.at[layer, second, 0], relay_send)
                await_bytes(landing.at[layer, first, :, 0], relay_send)
                await_bytes(landing.at[layer, 2, 0], relay_send)
                await_bytes(landing.at[layer, 0, :, 0], relay_send)
            await_bytes(landing.at[layer], relay_send)

    @pl.when(is_consumer)
    def _():
        position = src_ref[j * secs + q]
        layer_of = position // (size * size)
        inside = position - layer_of * (size * size)
        row_of = inside // size
        column_of = inside - row_of * size
        column_ids = lax.broadcasted_iota(jnp.int32, (1, size), 1)
        on_column = jnp.where(column_ids == column_of, 1.0, 0.0).astype(f32)

        def dot(a, b):
            return jnp.dot(a, b, preferred_element_type=f32)

        def dot_turned(a, b):
            return lax.dot_general(a, b, (((1,), (1,)), ((), ())), preferred_element_type=f32)

        def front(layer, source):
            vr = source[0]
            vi = source[1]
            yr = factor[layer, 2]
            yi = factor[layer, 3]
            turned[0] = (dot_turned(vr, yr) - dot_turned(vi, yi)).astype(bf16)
            turned[1] = (dot_turned(vr, yi) + dot_turned(vi, yr)).astype(bf16)
            xr = factor[layer, 0]
            xi = factor[layer, 1]
            real = dot(xr, turned[0]) - dot(xi, turned[1])
            yield 0, real
            yield 1, dot(xr, turned[1]) + dot(xi, turned[0])

        def gather_rows(layer, planes):
            def step(k, carry):
                outer = k // grid_y
                slot = lax.rem(k, grid_y)
                for m in planes:
                    tile = jnp.concatenate(
                        [landing[layer, m, outer, i, slot] for i in range(grid_y)], axis=0
                    )
                    factor[layer, m, pl.ds(pl.multiple_of(k * 32, 32), 32), :] = tile
                return carry

            lax.fori_loop(0, size // 32, step, 0)

        def emit(layer):
            def one(k, carry):
                piece = field.at[layer, :, pl.ds(pl.multiple_of(k * rows, rows), rows), :]
                target = out_ref.at[:, 0, :, pl.ds(pl.multiple_of(q * size, size), size)]
                here = (layer == q) & (k == p)

                @pl.when(here)
                def _():
                    pltpu.make_async_copy(piece, target, out_sem).start()

                @pl.when(jnp.logical_not(here))
                def _():
                    pltpu.make_async_remote_copy(
                        src_ref=piece, dst_ref=target, send_sem=out_send, recv_sem=out_sem,
                        device_id=(layer, k, j), device_id_type=MESH,
                    ).start()

                return carry

            lax.fori_loop(0, columns, one, 0)

        def forward(layer, carry):
            await_bytes(field.at[layer], field_sem.at[layer])
            strength = jnp.where(layer_of == layer, source_amplitude, 0.0).astype(f32)

            def reduce_rows(k, coupled):
                part = pl.ds(pl.multiple_of(k * 32, 32), 32)
                hit = lax.broadcasted_iota(jnp.int32, (32, 1), 0) == row_of - k * 32
                bump = jnp.where(hit, strength, 0.0) * on_column
                real = field[layer, 0, part, :].astype(f32) + bump
                imag = field[layer, 1, part, :].astype(f32)
                if coupled:
                    scale = weights[layer, part, :].astype(f32)
                    real = real - scale * field[layer - 1, 0, part, :].astype(f32)
                    imag = imag - scale * field[layer - 1, 1, part, :].astype(f32)
                sent[0, part, :] = real.astype(bf16)
                sent[1, part, :] = imag.astype(bf16)

            def sweep_rows(coupled):
                def step(k, carry):
                    reduce_rows(k, coupled)
                    return carry

                lax.fori_loop(0, size // 32, step, 0, unroll=2)

            @pl.when(layer == 0)
            def _():
                sweep_rows(False)

            @pl.when(layer > 0)
            def _():
                await_bytes(weights.at[layer], weight_sem.at[layer])
                sweep_rows(True)

            await_bytes(landing.at[layer, pl.ds(2, 2)], plane_sem.at[1, layer])
            gather_rows(layer, (2, 3))
            await_bytes(landing.at[layer, pl.ds(0, 2)], plane_sem.at[0, layer])
            gather_rows(layer, (0, 1))
            for plane, value in front(layer, sent):
                field[layer, plane] = value.astype(bf16)
            return carry

        lax.fori_loop(0, secs, forward, 0)
        emit(secs - 1)

        def backward(step, carry):
            layer = secs - 2 - step

            def couple_rows(k, carry):
                part = pl.ds(pl.multiple_of(k * 32, 32), 32)
                scale = weights[layer + 1, part, :].astype(f32)
                for m in range(2):
                    sent[m, part, :] = (scale * field[layer + 1, m, part, :].astype(f32)).astype(bf16)
                return carry

            lax.fori_loop(0, size // 32, couple_rows, 0, unroll=2)
            for plane, value in front(layer, sent):
                solved = value.astype(bf16).astype(f32)
                field[layer, plane] = (field[layer, plane].astype(f32) - solved).astype(bf16)
            emit(layer)
            return carry

        lax.fori_loop(0, secs - 1, backward, 0)
        await_bytes(field.at[pl.ds(0, secs - 1)], out_send)
        await_bytes(field.at[0, :, pl.ds(0, size - rows), :], out_send)

    @pl.when(jnp.logical_not(is_own_hub))
    def _():
        await_bytes(landing.at[0, :, 0, 0, 0], block_send)

    await_bytes(stage.at[pl.ds(0, secs - 1)], swap_send)

    @pl.when(q > 0)
    def _():
        await_bytes(stage_w.at[pl.ds(0, secs - 1)], swap_send)

    @pl.when(jnp.logical_not(is_consumer))
    def _():
        await_bytes(stage, field_send)
        await_bytes(stage_w.at[pl.ds(0, secs - 1)], field_send)

    await_bytes(out_ref, out_sem)


def solution(mesh):
    secs = mesh.shape["sec"]
    columns = mesh.shape["px"]
    grid_y = mesh.shape["py"]

    def on_device(background, src_pos, coupling, x_factor, y_factor):
        size = x_factor.shape[3]
        height = x_factor.shape[2]
        dims = (secs, columns, grid_y, size)

        def body(*refs):
            sweep_kernel(dims, *refs)

        any_spec = pl.BlockSpec(memory_space=pl.ANY)
        dma = pltpu.SemaphoreType.DMA
        return pl.pallas_call(
            body,
            out_shape=jax.ShapeDtypeStruct(background.shape, bf16),
            in_specs=[pl.BlockSpec(memory_space=pltpu.SMEM)] + [any_spec] * 4,
            out_specs=any_spec,
            scratch_shapes=[
                pltpu.VMEM((secs, 4, columns // grid_y, grid_y, grid_y, height, size), bf16),
                pltpu.VMEM((secs, 2, size // columns, size), bf16),
                pltpu.VMEM((secs, size // columns, size), bf16),
                pltpu.VMEM((secs, 4, size, size), bf16),
                pltpu.VMEM((secs, 2, size, size), bf16),
                pltpu.VMEM((secs, size, size), bf16),
                pltpu.VMEM((2, size, size), bf16),
                pltpu.VMEM((2, size, size), bf16),
                dma, dma, dma, dma, dma,
                dma((secs,)), dma((secs,)), dma((secs,)), dma((10, secs)), dma((2, secs)),
                dma((secs,)), dma((secs,)), dma,
            ],
            compiler_params=pltpu.CompilerParams(
                collective_id=0, has_side_effects=True, vmem_limit_bytes=60 * 2**20
            ),
            name="sweep",
        )(src_pos, background, coupling, x_factor, y_factor)

    placed = (
        P(None, "sec", "px", "py"),
        P(),
        P("sec", "px", None),
        P("sec", None, ("px", "py"), None),
        P("sec", None, ("px", "py"), None),
    )
    return jax.shard_map(
        on_device, mesh=mesh, in_specs=placed, out_specs=P(None, "sec", "px", "py"), check_vma=False
    )
```

```python
import jax
import jax.numpy as jnp
from jax import lax
from jax.experimental import pallas as pl
from jax.experimental.pallas import tpu as pltpu
from jax.sharding import PartitionSpec as P

MESH = pl.DeviceIdType.MESH
source_amplitude = 8.0
f32 = jnp.float32
bf16 = jnp.bfloat16


def sweep_kernel(
    dims, src_ref, bg_ref, cp_ref, xf_ref, yf_ref, out_ref,
    landing, stage, stage_w, factor, field, weights, sent, turned,
    block_send, swap_send, field_send, relay_send, out_send,
    block_sem, swap_sem, swap_w_sem, ring_sem, plane_sem, field_sem, weight_sem, out_sem,
):
    secs, columns, grid_y, size = dims
    rows = size // columns
    q = lax.axis_index("sec")
    p = lax.axis_index("px")
    j = lax.axis_index("py")
    group = p // grid_y
    inner = lax.rem(p, grid_y)
    is_consumer = p == 0
    is_relay = p == 1
    hub = (group, 1, j)
    is_own_hub = is_relay & (q == group)

    barrier = pltpu.get_barrier_semaphore()

    def greet(device):
        pl.semaphore_signal(barrier, inc=1, device_id=device, device_id_type=MESH)

    for step in range(1, secs):
        greet((lax.rem(q + step, secs), p, j))

    @pl.when(is_relay)
    def _():
        def tell(i, carry):
            greet((i // grid_y, q * grid_y + lax.rem(i, grid_y), j))
            return carry

        lax.fori_loop(0, secs * grid_y, tell, 0)
        for step in range(1, secs):
            greet((lax.rem(q + step, secs), 1, j))
        for step in range(1, grid_y):
            greet((q, 1, lax.rem(j + step, grid_y)))

    @pl.when(is_consumer)
    def _():
        def tell(i, carry):
            greet((q, i, j))
            return carry

        lax.fori_loop(0, columns, tell, 0)

    for a in range(secs):
        greet((a, 0, j))

    expected = secs + 1 + jnp.where(is_consumer, secs * columns, 0)
    expected = expected + jnp.where(is_relay, secs + grid_y - 2, 0)
    pl.semaphore_wait(barrier, expected)

    def await_bytes(ref, sem):
        pltpu.make_async_copy(ref, ref, sem).wait()

    def send(src, dst, send_sem, recv_sem, device):
        pltpu.make_async_remote_copy(
            src_ref=src, dst_ref=dst, send_sem=send_sem, recv_sem=recv_sem,
            device_id=device, device_id_type=MESH,
        ).start()

    def push(src, dst, send_sem, recv_sem, device, is_self):
        @pl.when(is_self)
        def _():
            pltpu.make_async_copy(src, dst, recv_sem).start()

        @pl.when(jnp.logical_not(is_self))
        def _():
            send(src, dst, send_sem, recv_sem, device)

    push(
        yf_ref.at[0], landing.at[q, pl.ds(2, 2), group, j, inner], block_send, block_sem.at[q],
        hub, is_own_hub,
    )
    push(
        xf_ref.at[0], landing.at[q, pl.ds(0, 2), group, j, inner], block_send, block_sem.at[q],
        hub, is_own_hub,
    )

    def source_block(a):
        return bg_ref.at[:, 0, :, pl.ds(pl.multiple_of(a * size, size), size)]

    for step in range(1, secs):
        a = lax.rem(q + step, secs)
        send(source_block(a), stage.at[q], swap_send, swap_sem.at[q], (a, p, j))

        @pl.when(q > 0)
        def _():
            send(cp_ref.at[0], stage_w.at[q], swap_send, swap_w_sem.at[q], (a, p, j))

    for layer in range(secs):

        @pl.when(q != layer)
        def _():
            await_bytes(stage.at[layer], swap_sem.at[layer])
            if layer:
                await_bytes(stage_w.at[layer], swap_w_sem.at[layer])

    own = pl.ds(pl.multiple_of(p * rows, rows), rows)
    home = (q, 0, j)
    for layer in range(secs):

        @pl.when(q == layer)
        def _():
            push(
                source_block(q), field.at[layer, :, own, :], field_send, field_sem.at[layer],
                home, is_consumer,
            )
            if layer:
                push(
                    cp_ref.at[0], weights.at[layer, own, :], field_send, weight_sem.at[layer],
                    home, is_consumer,
                )

        @pl.when(q != layer)
        def _():
            push(
                stage.at[layer], field.at[layer, :, own, :], field_send, field_sem.at[layer],
                home, is_consumer,
            )
            if layer:
                push(
                    stage_w.at[layer], weights.at[layer, own, :], field_send, weight_sem.at[layer],
                    home, is_consumer,
                )

    @pl.when(is_relay)
    def _():
        xs = [lax.rem(q + step, secs) for step in range(secs)]
        ys = [lax.rem(j + step, grid_y) for step in range(grid_y)]
        first = pl.ds(0, 2)
        second = pl.ds(2, 2)

        def open_layer(layer):
            await_bytes(landing.at[layer, :, 0, 0], block_sem.at[layer])
            piece = landing.at[layer, second, q, j]
            for y in ys[1:]:
                send(piece, piece, relay_send, ring_sem.at[0, layer], (q, 1, y))
            piece = landing.at[layer, first, q, j]
            for x in xs[1:]:
                send(piece, piece, relay_send, ring_sem.at[1, layer], (x, 1, j))

        def share(layer):
            await_bytes(landing.at[layer, second, 0, pl.ds(0, grid_y - 1)], ring_sem.at[0, layer])
            piece = landing.at[layer, second, q]
            send(piece, piece, relay_send, ring_sem.at[2, layer], (xs[1], 1, j))
            send(piece, piece, relay_send, ring_sem.at[3, layer], (xs[-1], 1, j))
            await_bytes(landing.at[layer, first, pl.ds(0, secs - 1), 0], ring_sem.at[1, layer])
            piece = landing.at[layer, first, :, j]
            send(piece, piece, relay_send, ring_sem.at[4, layer], (q, 1, ys[1]))
            send(piece, piece, relay_send, ring_sem.at[5, layer], (q, 1, ys[-1]))

        def relay(layer):
            await_bytes(landing.at[layer, second, 0], ring_sem.at[2, layer])
            piece = landing.at[layer, 2, xs[-1]]
            send(piece, piece, relay_send, ring_sem.at[6, layer], (xs[1], 1, j))
            await_bytes(landing.at[layer, second, 0], ring_sem.at[3, layer])
            piece = landing.at[layer, 3, xs[1]]
            send(piece, piece, relay_send, ring_sem.at[7, layer], (xs[-1], 1, j))
            await_bytes(landing.at[layer, first, :, 0], ring_sem.at[4, layer])
            piece = landing.at[layer, 0, :, ys[-1]]
            send(piece, piece, relay_send, ring_sem.at[8, layer], (q, 1, ys[1]))
            await_bytes(landing.at[layer, first, :, 0], ring_sem.at[5, layer])
            piece = landing.at[layer, 1, :, ys[1]]
            send(piece, piece, relay_send, ring_sem.at[9, layer], (q, 1, ys[-1]))

        def close_layer(layer):
            await_bytes(landing.at[layer, 2, 0], ring_sem.at[6, layer])
            await_bytes(landing.at[layer, 3, 0], ring_sem.at[7, layer])
            piece = landing.at[layer, second]
            send(piece, piece, relay_send, plane_sem.at[1, layer], home)
            await_bytes(landing.at[layer, 0, :, 0], ring_sem.at[8, layer])
            await_bytes(landing.at[layer, 1, :, 0], ring_sem.at[9, layer])
            piece = landing.at[layer, first]
            send(piece, piece, relay_send, plane_sem.at[0, layer], home)

        for tick in range(secs + 3):
            if tick == 0:
                for layer in range(secs):
                    open_layer(layer)
            if tick < secs:
                share(tick)
            if 1 <= tick <= secs:
                relay(tick - 1)
            if 2 <= tick <= secs + 1:
                close_layer(tick - 2)
        for layer in range(secs):
            for step in range(1, secs):
                await_bytes(landing.at[layer, second, 0, 0], relay_send)
                await_bytes(landing.at[layer, first, 0, 0], relay_send)
            for side in range(2):
                await_bytes(landing.at[layer, second, 0], relay_send)
                await_bytes(landing.at[layer, first, :, 0], relay_send)
                await_bytes(landing.at[layer, 2, 0], relay_send)
                await_bytes(landing.at[layer, 0, :, 0], relay_send)
            await_bytes(landing.at[layer], relay_send)

    @pl.when(is_consumer)
    def _():
        position = src_ref[j * secs + q]
        layer_of = position // (size * size)
        inside = position - layer_of * (size * size)
        row_of = inside // size
        column_of = inside - row_of * size
        column_ids = lax.broadcasted_iota(jnp.int32, (1, size), 1)
        on_column = jnp.where(column_ids == column_of, 1.0, 0.0).astype(f32)

        def dot(a, b):
            return jnp.dot(a, b, preferred_element_type=f32)

        def dot_turned(a, b):
            return lax.dot_general(a, b, (((1,), (1,)), ((), ())), preferred_element_type=f32)

        def front(layer, source):
            vr = source[0]
            vi = source[1]
            yr = factor[layer, 2]
            yi = factor[layer, 3]
            turned[0] = (dot_turned(vr, yr) - dot_turned(vi, yi)).astype(bf16)
            turned[1] = (dot_turned(vr, yi) + dot_turned(vi, yr)).astype(bf16)
            xr = factor[layer, 0]
            xi = factor[layer, 1]
            real = dot(xr, turned[0]) - dot(xi, turned[1])
            yield 0, real
            yield 1, dot(xr, turned[1]) + dot(xi, turned[0])

        def gather_rows(layer, planes):
            def step(k, carry):
                outer = k // grid_y
                slot = lax.rem(k, grid_y)
                for m in planes:
                    tile = jnp.concatenate(
                        [landing[layer, m, outer, i, slot] for i in range(grid_y)], axis=0
                    )
                    factor[layer, m, pl.ds(pl.multiple_of(k * 32, 32), 32), :] = tile
                return carry

            lax.fori_loop(0, size // 32, step, 0)

        def emit(layer):
            def one(k, carry):
                piece = field.at[layer, :, pl.ds(pl.multiple_of(k * rows, rows), rows), :]
                target = out_ref.at[:, 0, :, pl.ds(pl.multiple_of(q * size, size), size)]
                here = (layer == q) & (k == p)

                @pl.when(here)
                def _():
                    pltpu.make_async_copy(piece, target, out_sem).start()

                @pl.when(jnp.logical_not(here))
                def _():
                    pltpu.make_async_remote_copy(
                        src_ref=piece, dst_ref=target, send_sem=out_send, recv_sem=out_sem,
                        device_id=(layer, k, j), device_id_type=MESH,
                    ).start()

                return carry

            lax.fori_loop(0, columns, one, 0)

        def forward(layer, carry):
            await_bytes(field.at[layer], field_sem.at[layer])
            strength = jnp.where(layer_of == layer, source_amplitude, 0.0).astype(f32)

            def reduce_rows(k, coupled):
                part = pl.ds(pl.multiple_of(k * 32, 32), 32)
                hit = lax.broadcasted_iota(jnp.int32, (32, 1), 0) == row_of - k * 32
                bump = jnp.where(hit, strength, 0.0) * on_column
                real = field[layer, 0, part, :].astype(f32) + bump
                imag = field[layer, 1, part, :].astype(f32)
                if coupled:
                    scale = weights[layer, part, :].astype(f32)
                    real = real - scale * field[layer - 1, 0, part, :].astype(f32)
                    imag = imag - scale * field[layer - 1, 1, part, :].astype(f32)
                sent[0, part, :] = real.astype(bf16)
                sent[1, part, :] = imag.astype(bf16)

            def sweep_rows(coupled):
                def step(k, carry):
                    reduce_rows(k, coupled)
                    return carry

                lax.fori_loop(0, size // 32, step, 0, unroll=2)

            @pl.when(layer == 0)
            def _():
                sweep_rows(False)

            @pl.when(layer > 0)
            def _():
                await_bytes(weights.at[layer], weight_sem.at[layer])
                sweep_rows(True)

            await_bytes(landing.at[layer, pl.ds(2, 2)], plane_sem.at[1, layer])
            gather_rows(layer, (2, 3))
            await_bytes(landing.at[layer, pl.ds(0, 2)], plane_sem.at[0, layer])
            gather_rows(layer, (0, 1))
            for plane, value in front(layer, sent):
                field[layer, plane] = value.astype(bf16)
            return carry

        lax.fori_loop(0, secs, forward, 0)
        emit(secs - 1)

        def backward(step, carry):
            layer = secs - 2 - step

            def couple_rows(k, carry):
                part = pl.ds(pl.multiple_of(k * 32, 32), 32)
                scale = weights[layer + 1, part, :].astype(f32)
                for m in range(2):
                    sent[m, part, :] = (scale * field[layer + 1, m, part, :].astype(f32)).astype(bf16)
                return carry

            lax.fori_loop(0, size // 32, couple_rows, 0, unroll=2)
            for plane, value in front(layer, sent):
                solved = value.astype(bf16).astype(f32)
                field[layer, plane] = (field[layer, plane].astype(f32) - solved).astype(bf16)
            emit(layer)
            return carry

        lax.fori_loop(0, secs - 1, backward, 0)
        await_bytes(field.at[pl.ds(0, secs - 1)], out_send)
        await_bytes(field.at[0, :, pl.ds(0, size - rows), :], out_send)

    @pl.when(jnp.logical_not(is_own_hub))
    def _():
        await_bytes(landing.at[0, :, 0, 0, 0], block_send)

    await_bytes(stage.at[pl.ds(0, secs - 1)], swap_send)

    @pl.when(q > 0)
    def _():
        await_bytes(stage_w.at[pl.ds(0, secs - 1)], swap_send)

    @pl.when(jnp.logical_not(is_consumer))
    def _():
        await_bytes(stage, field_send)
        await_bytes(stage_w.at[pl.ds(0, secs - 1)], field_send)

    await_bytes(out_ref, out_sem)


def solution(mesh):
    secs = mesh.shape["sec"]
    columns = mesh.shape["px"]
    grid_y = mesh.shape["py"]

    def on_device(background, src_pos, coupling, x_factor, y_factor):
        size = x_factor.shape[3]
        height = x_factor.shape[2]
        dims = (secs, columns, grid_y, size)

        def body(*refs):
            sweep_kernel(dims, *refs)

        any_spec = pl.BlockSpec(memory_space=pl.ANY)
        dma = pltpu.SemaphoreType.DMA
        return pl.pallas_call(
            body,
            out_shape=jax.ShapeDtypeStruct(background.shape, bf16),
            in_specs=[pl.BlockSpec(memory_space=pltpu.SMEM)] + [any_spec] * 4,
            out_specs=any_spec,
            scratch_shapes=[
                pltpu.VMEM((secs, 4, columns // grid_y, grid_y, grid_y, height, size), bf16),
                pltpu.VMEM((secs, 2, size // columns, size), bf16),
                pltpu.VMEM((secs, size // columns, size), bf16),
                pltpu.VMEM((secs, 4, size, size), bf16),
                pltpu.VMEM((secs, 2, size, size), bf16),
                pltpu.VMEM((secs, size, size), bf16),
                pltpu.VMEM((2, size, size), bf16),
                pltpu.VMEM((2, size, size), bf16),
                dma, dma, dma, dma, dma,
                dma((secs,)), dma((secs,)), dma((secs,)), dma((10, secs)), dma((2, secs)),
                dma((secs,)), dma((secs,)), dma,
            ],
            compiler_params=pltpu.CompilerParams(
                collective_id=0, has_side_effects=True, vmem_limit_bytes=60 * 2**20
            ),
            name="sweep",
        )(src_pos, background, coupling, x_factor, y_factor)

    placed = (
        P(None, "sec", "px", "py"),
        P(),
        P("sec", "px", None),
        P("sec", None, ("px", "py"), None),
        P("sec", None, ("px", "py"), None),
    )
    return jax.shard_map(
        on_device, mesh=mesh, in_specs=placed, out_specs=P(None, "sec", "px", "py"), check_vma=False
    )
```

```python
import jax
import jax.numpy as jnp
from jax import lax
from jax.experimental import pallas as pl
from jax.experimental.pallas import tpu as pltpu
from jax.sharding import PartitionSpec as P

MESH = pl.DeviceIdType.MESH
source_amplitude = 8.0
f32 = jnp.float32
bf16 = jnp.bfloat16


def sweep_kernel(
    dims, src_ref, bg_ref, cp_ref, xf_ref, yf_ref, out_ref,
    landing, stage, stage_w, factor, field, weights, sent, turned,
    block_send, swap_send, field_send, relay_send, out_send,
    block_sem, swap_sem, swap_w_sem, ring_sem, plane_sem, field_sem, weight_sem, out_sem,
    hop, hop_w, hop_out, hop_send, hop_sem, hop_w_sem, hop_out_sem, go_sem,
):
    secs, columns, grid_y, size = dims
    rows = size // columns
    q = lax.axis_index("sec")
    p = lax.axis_index("px")
    j = lax.axis_index("py")
    group = p // grid_y
    inner = lax.rem(p, grid_y)
    is_consumer = p == 0
    is_relay = p == 1
    hub = (group, 1, j)
    quarter = columns // 4
    is_near = ((p >= 2) & (p < 2 + quarter)) | (p >= columns - quarter)
    detour = columns // 2 + 1
    helper = columns // 2 - 1
    out_helper = columns // 2 + 3
    is_own_hub = is_relay & (q == group)

    barrier = pltpu.get_barrier_semaphore()

    def greet(device):
        pl.semaphore_signal(barrier, inc=1, device_id=device, device_id_type=MESH)

    for step in range(1, secs):
        greet((lax.rem(q + step, secs), p, j))

    @pl.when(is_relay)
    def _():
        def tell(i, carry):
            greet((i // grid_y, q * grid_y + lax.rem(i, grid_y), j))
            return carry

        lax.fori_loop(0, secs * grid_y, tell, 0)
        for step in range(1, secs):
            greet((lax.rem(q + step, secs), 1, j))
        for step in range(1, grid_y):
            greet((q, 1, lax.rem(j + step, grid_y)))

    @pl.when(is_consumer)
    def _():
        def tell(i, carry):
            greet((q, i, j))
            return carry

        lax.fori_loop(0, columns, tell, 0)

    for a in range(secs):
        greet((a, 0, j))

    @pl.when(p == helper)
    def _():
        greet((q, detour, j))

    @pl.when(p == detour)
    def _():
        for a in range(secs):
            greet((a, out_helper, j))

    expected = secs + 1 + jnp.where(is_consumer, secs * columns, 0)
    expected = expected + jnp.where(is_relay, secs + grid_y - 2, 0)
    expected = expected + jnp.where(p == detour, 1, 0)
    expected = expected + jnp.where(p == out_helper, secs, 0)
    pl.semaphore_wait(barrier, expected)

    def await_bytes(ref, sem):
        pltpu.make_async_copy(ref, ref, sem).wait()

    def send(src, dst, send_sem, recv_sem, device):
        pltpu.make_async_remote_copy(
            src_ref=src, dst_ref=dst, send_sem=send_sem, recv_sem=recv_sem,
            device_id=device, device_id_type=MESH,
        ).start()

    def push(src, dst, send_sem, recv_sem, device, is_self):
        @pl.when(is_self)
        def _():
            pltpu.make_async_copy(src, dst, recv_sem).start()

        @pl.when(jnp.logical_not(is_self))
        def _():
            send(src, dst, send_sem, recv_sem, device)

    push(
        yf_ref.at[0], landing.at[q, pl.ds(2, 2), group, j, inner], block_send, block_sem.at[q],
        hub, is_own_hub,
    )
    push(
        xf_ref.at[0], landing.at[q, pl.ds(0, 2), group, j, inner], block_send, block_sem.at[q],
        hub, is_own_hub,
    )

    def source_block_of(ref, a):
        return ref.at[:, 0, :, pl.ds(pl.multiple_of(a * size, size), size)]

    def source_block(a):
        return source_block_of(bg_ref, a)

    for step in range(1, secs):
        a = lax.rem(q + step, secs)
        send(source_block(a), stage.at[q], swap_send, swap_sem.at[q], (a, p, j))

    @pl.when(q > 0)
    def _():
        for step in range(1, secs):
            a = lax.rem(q + step, secs)
            send(cp_ref.at[0], stage_w.at[q], swap_send, swap_w_sem.at[q], (a, p, j))

    for layer in range(secs):

        @pl.when(q != layer)
        def _():
            await_bytes(stage.at[layer], swap_sem.at[layer])

    home = (q, 0, j)
    half = jnp.where(is_near, 1, 0)

    @pl.when(is_near)
    def _():
        pl.semaphore_wait(go_sem, 1)

    def rows_of(k):
        return pl.ds(pl.multiple_of(k * rows, rows), rows)

    def pass_on(layer, block, block_w):
        @pl.when(p == detour)
        def _():
            send(block, hop.at[layer], field_send.at[layer], hop_sem.at[layer], (q, helper, j))

        @pl.when(p != detour)
        def _():
            push(
                block, field.at[layer, :, rows_of(p), :], field_send.at[layer], field_sem.at[half, layer],
                home, is_consumer,
            )

        if layer:

            @pl.when(q != layer)
            def _():
                await_bytes(stage_w.at[layer], swap_w_sem.at[layer])

            @pl.when(p == detour)
            def _():
                send(block_w, hop_w.at[layer], field_send.at[layer], hop_w_sem.at[layer], (q, helper, j))

            @pl.when(p != detour)
            def _():
                push(
                    block_w, weights.at[layer, rows_of(p), :], field_send.at[layer],
                    weight_sem.at[half, layer], home, is_consumer,
                )

    def await_sent(layer):
        @pl.when(jnp.logical_not(is_consumer))
        def _():
            await_bytes(stage.at[layer], field_send.at[layer])
            if layer:
                await_bytes(stage_w.at[layer], field_send.at[layer])

    for layer in range(secs):
        if layer >= 1:
            await_sent(layer - 1)

        @pl.when(q == layer)
        def _():
            pass_on(layer, source_block(q), cp_ref.at[0])

        @pl.when(q != layer)
        def _():
            pass_on(layer, stage.at[layer], stage_w.at[layer])

    @pl.when(p == helper)
    def _():
        for layer in range(secs):
            await_bytes(hop.at[layer], hop_sem.at[layer])
            send(
                hop.at[layer], field.at[layer, :, pl.ds(detour * rows, rows), :], hop_send,
                field_sem.at[0, layer], home,
            )
            if layer:
                await_bytes(hop_w.at[layer], hop_w_sem.at[layer])
                send(
                    hop_w.at[layer], weights.at[layer, pl.ds(detour * rows, rows), :], hop_send,
                    weight_sem.at[0, layer], home,
                )

    @pl.when(is_relay)
    def _():
        xs = [lax.rem(q + step, secs) for step in range(secs)]
        ys = [lax.rem(j + step, grid_y) for step in range(grid_y)]
        first = pl.ds(0, 2)
        second = pl.ds(2, 2)

        def deliver(piece, part, layer):
            send(piece, piece, relay_send, plane_sem.at[part, layer], home)

        def open_layer(layer):
            await_bytes(landing.at[layer, :, 0, 0], block_sem.at[layer])
            piece = landing.at[layer, second, q, j]
            for y in ys[1:]:
                send(piece, piece, relay_send, ring_sem.at[0, layer], (q, 1, y))
            piece = landing.at[layer, first, q, j]
            for x in xs[1:]:
                send(piece, piece, relay_send, ring_sem.at[1, layer], (x, 1, j))

        def share(layer):
            await_bytes(landing.at[layer, second, 0, pl.ds(0, grid_y - 1)], ring_sem.at[0, layer])
            piece = landing.at[layer, second, q]
            send(piece, piece, relay_send, ring_sem.at[2, layer], (xs[1], 1, j))
            send(piece, piece, relay_send, ring_sem.at[3, layer], (xs[-1], 1, j))
            deliver(piece, 1, layer)
            await_bytes(landing.at[layer, first, pl.ds(0, secs - 1), 0], ring_sem.at[1, layer])
            piece = landing.at[layer, first, :, j]
            send(piece, piece, relay_send, ring_sem.at[4, layer], (q, 1, ys[1]))
            send(piece, piece, relay_send, ring_sem.at[5, layer], (q, 1, ys[-1]))
            deliver(piece, 0, layer)

        def relay(layer):
            await_bytes(landing.at[layer, second, 0], ring_sem.at[2, layer])
            piece = landing.at[layer, 2, xs[-1]]
            send(piece, piece, relay_send, ring_sem.at[6, layer], (xs[1], 1, j))
            deliver(landing.at[layer, second, xs[-1]], 1, layer)
            await_bytes(landing.at[layer, second, 0], ring_sem.at[3, layer])
            piece = landing.at[layer, 3, xs[1]]
            send(piece, piece, relay_send, ring_sem.at[7, layer], (xs[-1], 1, j))
            deliver(landing.at[layer, second, xs[1]], 1, layer)
            await_bytes(landing.at[layer, first, :, 0], ring_sem.at[4, layer])
            piece = landing.at[layer, 0, :, ys[-1]]
            send(piece, piece, relay_send, ring_sem.at[8, layer], (q, 1, ys[1]))
            deliver(landing.at[layer, first, :, ys[-1]], 0, layer)
            await_bytes(landing.at[layer, first, :, 0], ring_sem.at[5, layer])
            piece = landing.at[layer, 1, :, ys[1]]
            send(piece, piece, relay_send, ring_sem.at[9, layer], (q, 1, ys[-1]))
            deliver(landing.at[layer, first, :, ys[1]], 0, layer)

        def close_layer(layer):
            await_bytes(landing.at[layer, 2, 0], ring_sem.at[6, layer])
            await_bytes(landing.at[layer, 3, 0], ring_sem.at[7, layer])
            deliver(landing.at[layer, second, xs[2]], 1, layer)
            await_bytes(landing.at[layer, 0, :, 0], ring_sem.at[8, layer])
            await_bytes(landing.at[layer, 1, :, 0], ring_sem.at[9, layer])
            deliver(landing.at[layer, first, :, ys[2]], 0, layer)

        for tick in range(secs + 3):
            if tick == 0:
                for layer in range(secs):
                    open_layer(layer)
            if tick < secs:
                share(tick)
            if 1 <= tick <= secs:
                relay(tick - 1)
            if 2 <= tick <= secs + 1:
                close_layer(tick - 2)
        for layer in range(secs):
            for step in range(1, secs):
                await_bytes(landing.at[layer, second, 0, 0], relay_send)
                await_bytes(landing.at[layer, first, 0, 0], relay_send)
            for side in range(2):
                await_bytes(landing.at[layer, second, 0], relay_send)
                await_bytes(landing.at[layer, first, :, 0], relay_send)
                await_bytes(landing.at[layer, 2, 0], relay_send)
                await_bytes(landing.at[layer, 0, :, 0], relay_send)
            await_bytes(landing.at[layer], relay_send)

    @pl.when(is_consumer)
    def _():
        position = src_ref[j * secs + q]
        layer_of = position // (size * size)
        inside = position - layer_of * (size * size)
        row_of = inside // size
        column_of = inside - row_of * size
        column_ids = lax.broadcasted_iota(jnp.int32, (1, size), 1)
        on_column = jnp.where(column_ids == column_of, 1.0, 0.0).astype(f32)

        def dot(a, b):
            return jnp.dot(a, b, preferred_element_type=f32)

        def dot_turned(a, b):
            return lax.dot_general(a, b, (((1,), (1,)), ((), ())), preferred_element_type=f32)

        def front(layer, source):
            vr = source[0]
            vi = source[1]
            yr = factor[layer, 2]
            yi = factor[layer, 3]
            turned[0] = (dot_turned(vr, yr) - dot_turned(vi, yi)).astype(bf16)
            turned[1] = (dot_turned(vr, yi) + dot_turned(vi, yr)).astype(bf16)
            xr = factor[layer, 0]
            xi = factor[layer, 1]
            real = dot(xr, turned[0]) - dot(xi, turned[1])
            yield 0, real
            yield 1, dot(xr, turned[1]) + dot(xi, turned[0])

        def gather_rows(layer, planes):
            def step(k, carry):
                outer = k // grid_y
                slot = lax.rem(k, grid_y)
                for m in planes:
                    tile = jnp.concatenate(
                        [landing[layer, m, outer, i, slot] for i in range(grid_y)], axis=0
                    )
                    factor[layer, m, pl.ds(pl.multiple_of(k * 32, 32), 32), :] = tile
                return carry

            lax.fori_loop(0, size // 32, step, 0)

        def emit(layer):
            def one(k, carry):
                piece = field.at[layer, :, pl.ds(pl.multiple_of(k * rows, rows), rows), :]
                target = out_ref.at[:, 0, :, pl.ds(pl.multiple_of(q * size, size), size)]
                here = (layer == q) & (k == p)

                @pl.when(here)
                def _():
                    pltpu.make_async_copy(piece, target, out_sem).start()

                @pl.when(jnp.logical_not(here) & (k != detour))
                def _():
                    send(piece, target, out_send, out_sem, (layer, k, j))

                @pl.when(k == detour)
                def _():
                    send(piece, hop_out.at[layer], out_send, hop_out_sem.at[layer], (q, out_helper, j))

                return carry

            lax.fori_loop(0, columns, one, 0)

        half_rows = pl.ds(0, size // 2)

        def await_half(which, layer):
            await_bytes(field.at[layer, :, half_rows, :], field_sem.at[which, layer])

        def await_half_w(which, layer):
            await_bytes(weights.at[layer, half_rows, :], weight_sem.at[which, layer])

        for layer in range(1):
            await_half(0, layer)
            if layer:
                await_half_w(0, layer)
        for step in range(quarter):
            for k in (2 + step, columns - 1 - step):
                pl.semaphore_signal(go_sem, inc=1, device_id=(q, k, j), device_id_type=MESH)

        def forward(layer, carry):
            await_half(1, layer)

            @pl.when(layer > 0)
            def _():
                await_half(0, layer)
                await_half_w(0, layer)

            strength = jnp.where(layer_of == layer, source_amplitude, 0.0).astype(f32)

            def reduce_rows(k, coupled):
                part = pl.ds(pl.multiple_of(k * 32, 32), 32)
                hit = lax.broadcasted_iota(jnp.int32, (32, 1), 0) == row_of - k * 32
                bump = jnp.where(hit, strength, 0.0) * on_column
                real = field[layer, 0, part, :].astype(f32) + bump
                imag = field[layer, 1, part, :].astype(f32)
                if coupled:
                    scale = weights[layer, part, :].astype(f32)
                    real = real - scale * field[layer - 1, 0, part, :].astype(f32)
                    imag = imag - scale * field[layer - 1, 1, part, :].astype(f32)
                sent[0, part, :] = real.astype(bf16)
                sent[1, part, :] = imag.astype(bf16)

            def sweep_rows(coupled):
                def step(k, carry):
                    reduce_rows(k, coupled)
                    return carry

                lax.fori_loop(0, size // 32, step, 0, unroll=2)

            @pl.when(layer == 0)
            def _():
                sweep_rows(False)

            @pl.when(layer > 0)
            def _():
                await_half_w(1, layer)
                sweep_rows(True)

            await_bytes(landing.at[layer, pl.ds(2, 2)], plane_sem.at[1, layer])
            gather_rows(layer, (2, 3))
            await_bytes(landing.at[layer, pl.ds(0, 2)], plane_sem.at[0, layer])
            gather_rows(layer, (0, 1))
            for plane, value in front(layer, sent):
                field[layer, plane] = value.astype(bf16)
            return carry

        lax.fori_loop(0, secs, forward, 0)
        emit(secs - 1)

        def backward(step, carry):
            layer = secs - 2 - step

            def couple_rows(k, carry):
                part = pl.ds(pl.multiple_of(k * 32, 32), 32)
                scale = weights[layer + 1, part, :].astype(f32)
                for m in range(2):
                    sent[m, part, :] = (scale * field[layer + 1, m, part, :].astype(f32)).astype(bf16)
                return carry

            lax.fori_loop(0, size // 32, couple_rows, 0, unroll=2)
            for plane, value in front(layer, sent):
                solved = value.astype(bf16).astype(f32)
                field[layer, plane] = (field[layer, plane].astype(f32) - solved).astype(bf16)
            emit(layer)
            return carry

        lax.fori_loop(0, secs - 1, backward, 0)
        await_bytes(field.at[pl.ds(0, secs - 1)], out_send)
        await_bytes(field.at[0, :, pl.ds(0, size - rows), :], out_send)

    @pl.when(p == out_helper)
    def _():
        for layer in range(secs - 1, -1, -1):
            await_bytes(hop_out.at[layer], hop_out_sem.at[layer])
            send(hop_out.at[layer], source_block_of(out_ref, q), hop_send, out_sem, (layer, detour, j))
        await_bytes(hop_out, hop_send)

    @pl.when(jnp.logical_not(is_own_hub))
    def _():
        await_bytes(landing.at[0, :, 0, 0, 0], block_send)

    await_bytes(stage.at[pl.ds(0, secs - 1)], swap_send)

    @pl.when(q > 0)
    def _():
        await_bytes(stage_w.at[pl.ds(0, secs - 1)], swap_send)

    for layer in range(secs - 1, secs):
        await_sent(layer)

    @pl.when(p == helper)
    def _():
        await_bytes(hop, hop_send)
        await_bytes(hop_w.at[pl.ds(0, secs - 1)], hop_send)

    await_bytes(out_ref, out_sem)


def solution(mesh):
    secs = mesh.shape["sec"]
    columns = mesh.shape["px"]
    grid_y = mesh.shape["py"]

    def on_device(background, src_pos, coupling, x_factor, y_factor):
        size = x_factor.shape[3]
        height = x_factor.shape[2]
        dims = (secs, columns, grid_y, size)

        def body(*refs):
            sweep_kernel(dims, *refs)

        any_spec = pl.BlockSpec(memory_space=pl.ANY)
        dma = pltpu.SemaphoreType.DMA
        return pl.pallas_call(
            body,
            out_shape=jax.ShapeDtypeStruct(background.shape, bf16),
            in_specs=[pl.BlockSpec(memory_space=pltpu.SMEM)] + [any_spec] * 4,
            out_specs=any_spec,
            scratch_shapes=[
                pltpu.VMEM((secs, 4, columns // grid_y, grid_y, grid_y, height, size), bf16),
                pltpu.VMEM((secs, 2, size // columns, size), bf16),
                pltpu.VMEM((secs, size // columns, size), bf16),
                pltpu.VMEM((secs, 4, size, size), bf16),
                pltpu.VMEM((secs, 2, size, size), bf16),
                pltpu.VMEM((secs, size, size), bf16),
                pltpu.VMEM((2, size, size), bf16),
                pltpu.VMEM((2, size, size), bf16),
                dma, dma, dma((secs,)), dma, dma,
                dma((secs,)), dma((secs,)), dma((secs,)), dma((10, secs)), dma((2, secs)),
                dma((2, secs)), dma((2, secs)), dma,
                pltpu.VMEM((secs, 2, size // columns, size), bf16),
                pltpu.VMEM((secs, size // columns, size), bf16),
                pltpu.VMEM((secs, 2, size // columns, size), bf16),
                dma, dma((secs,)), dma((secs,)), dma((secs,)), pltpu.SemaphoreType.REGULAR,
            ],
            compiler_params=pltpu.CompilerParams(
                collective_id=0, has_side_effects=True, vmem_limit_bytes=60 * 2**20
            ),
            name="sweep",
        )(src_pos, background, coupling, x_factor, y_factor)

    placed = (
        P(None, "sec", "px", "py"),
        P(),
        P("sec", "px", None),
        P("sec", None, ("px", "py"), None),
        P("sec", None, ("px", "py"), None),
    )
    return jax.shard_map(
        on_device, mesh=mesh, in_specs=placed, out_specs=P(None, "sec", "px", "py"), check_vma=False
    )
```

```python
import jax
import jax.numpy as jnp
from jax import lax
from jax.experimental import pallas as pl
from jax.experimental.pallas import tpu as pltpu
from jax.sharding import PartitionSpec as P

MESH = pl.DeviceIdType.MESH
source_amplitude = 8.0
f32 = jnp.float32
bf16 = jnp.bfloat16


def sweep_kernel(
    dims, src_ref, bg_ref, cp_ref, xf_ref, yf_ref, out_ref,
    landing, stage, stage_w, factor, field, weights, sent, turned,
    block_send, swap_send, field_send, relay_send, out_send,
    block_sem, swap_sem, swap_w_sem, ring_sem, plane_sem, field_sem, weight_sem, out_sem,
    hop, hop_w, hop_out, hop_send, hop_sem, hop_w_sem, hop_out_sem, go_sem,
):
    secs, columns, grid_y, size = dims
    rows = size // columns
    q = lax.axis_index("sec")
    p = lax.axis_index("px")
    j = lax.axis_index("py")
    group = p // grid_y
    inner = lax.rem(p, grid_y)
    is_consumer = p == 0
    is_relay = p == 1
    hub = (group, 1, j)
    quarter = columns // 4
    is_near = ((p >= 2) & (p < 2 + quarter)) | (p >= columns - quarter)
    detour = columns // 2 + 1
    helper = columns // 2 - 1
    out_helper = columns // 2 + 3
    is_own_hub = is_relay & (q == group)

    barrier = pltpu.get_barrier_semaphore()

    def greet(device):
        pl.semaphore_signal(barrier, inc=1, device_id=device, device_id_type=MESH)

    for step in range(1, secs):
        greet((lax.rem(q + step, secs), p, j))

    @pl.when(is_relay)
    def _():
        def tell(i, carry):
            greet((i // grid_y, q * grid_y + lax.rem(i, grid_y), j))
            return carry

        lax.fori_loop(0, secs * grid_y, tell, 0)
        for step in range(1, secs):
            greet((lax.rem(q + step, secs), 1, j))
        for step in range(1, grid_y):
            greet((q, 1, lax.rem(j + step, grid_y)))

    @pl.when(is_consumer)
    def _():
        def tell(i, carry):
            greet((q, i, j))
            return carry

        lax.fori_loop(0, columns, tell, 0)

    for a in range(secs):
        greet((a, 0, j))

    @pl.when(p == helper)
    def _():
        greet((q, detour, j))

    @pl.when(p == detour)
    def _():
        for a in range(secs):
            greet((a, out_helper, j))

    expected = secs + 1 + jnp.where(is_consumer, secs * columns, 0)
    expected = expected + jnp.where(is_relay, secs + grid_y - 2, 0)
    expected = expected + jnp.where(p == detour, 1, 0)
    expected = expected + jnp.where(p == out_helper, secs, 0)
    pl.semaphore_wait(barrier, expected)

    def await_bytes(ref, sem):
        pltpu.make_async_copy(ref, ref, sem).wait()

    def send(src, dst, send_sem, recv_sem, device):
        pltpu.make_async_remote_copy(
            src_ref=src, dst_ref=dst, send_sem=send_sem, recv_sem=recv_sem,
            device_id=device, device_id_type=MESH,
        ).start()

    def push(src, dst, send_sem, recv_sem, device, is_self):
        @pl.when(is_self)
        def _():
            pltpu.make_async_copy(src, dst, recv_sem).start()

        @pl.when(jnp.logical_not(is_self))
        def _():
            send(src, dst, send_sem, recv_sem, device)

    push(
        yf_ref.at[0], landing.at[q, pl.ds(2, 2), group, j, inner], block_send, block_sem.at[q],
        hub, is_own_hub,
    )
    push(
        xf_ref.at[0], landing.at[q, pl.ds(0, 2), group, j, inner], block_send, block_sem.at[q],
        hub, is_own_hub,
    )

    def source_block_of(ref, a):
        return ref.at[:, 0, :, pl.ds(pl.multiple_of(a * size, size), size)]

    def source_block(a):
        return source_block_of(bg_ref, a)

    for step in range(1, secs):
        a = lax.rem(q + step, secs)
        send(source_block(a), stage.at[q], swap_send, swap_sem.at[q], (a, p, j))

    @pl.when(q > 0)
    def _():
        for step in range(1, secs):
            a = lax.rem(q + step, secs)
            send(cp_ref.at[0], stage_w.at[q], swap_send, swap_w_sem.at[q], (a, p, j))

    for layer in range(secs):

        @pl.when(q != layer)
        def _():
            await_bytes(stage.at[layer], swap_sem.at[layer])

    home = (q, 0, j)
    half = jnp.where(is_near, 1, 0)

    def rows_of(k):
        return pl.ds(pl.multiple_of(k * rows, rows), rows)

    def pass_on(layer, block, block_w):
        @pl.when(p == detour)
        def _():
            send(block, hop.at[layer], field_send.at[layer], hop_sem.at[layer], (q, helper, j))

        @pl.when(p != detour)
        def _():
            push(
                block, field.at[layer, :, rows_of(p), :], field_send.at[layer], field_sem.at[half, layer],
                home, is_consumer,
            )

        if layer:

            @pl.when(q != layer)
            def _():
                await_bytes(stage_w.at[layer], swap_w_sem.at[layer])

            @pl.when(p == detour)
            def _():
                send(block_w, hop_w.at[layer], field_send.at[layer], hop_w_sem.at[layer], (q, helper, j))

            @pl.when(p != detour)
            def _():
                push(
                    block_w, weights.at[layer, rows_of(p), :], field_send.at[layer],
                    weight_sem.at[half, layer], home, is_consumer,
                )

    def await_sent(layer):
        @pl.when(jnp.logical_not(is_consumer))
        def _():
            await_bytes(stage.at[layer], field_send.at[layer])
            if layer:
                await_bytes(stage_w.at[layer], field_send.at[layer])

    for layer in range(secs):

        if layer:

            @pl.when(is_near)
            def _():
                pl.semaphore_wait(go_sem, 1)

        if layer >= 2:

            @pl.when(jnp.logical_not(is_near))
            def _():
                await_sent(layer - 2)

        if layer >= 1:

            @pl.when(is_near)
            def _():
                await_sent(layer - 1)


        @pl.when(q == layer)
        def _():
            pass_on(layer, source_block(q), cp_ref.at[0])

        @pl.when(q != layer)
        def _():
            pass_on(layer, stage.at[layer], stage_w.at[layer])

    @pl.when(p == helper)
    def _():
        for layer in range(secs):
            await_bytes(hop.at[layer], hop_sem.at[layer])
            send(
                hop.at[layer], field.at[layer, :, pl.ds(detour * rows, rows), :], hop_send,
                field_sem.at[0, layer], home,
            )
            if layer:
                await_bytes(hop_w.at[layer], hop_w_sem.at[layer])
                send(
                    hop_w.at[layer], weights.at[layer, pl.ds(detour * rows, rows), :], hop_send,
                    weight_sem.at[0, layer], home,
                )

    @pl.when(is_relay)
    def _():
        xs = [lax.rem(q + step, secs) for step in range(secs)]
        ys = [lax.rem(j + step, grid_y) for step in range(grid_y)]
        first = pl.ds(0, 2)
        second = pl.ds(2, 2)

        def deliver(piece, part, layer):
            send(piece, piece, relay_send, plane_sem.at[part, layer], home)

        def open_layer(layer):
            await_bytes(landing.at[layer, :, 0, 0], block_sem.at[layer])
            piece = landing.at[layer, second, q, j]
            for y in ys[1:]:
                send(piece, piece, relay_send, ring_sem.at[0, layer], (q, 1, y))
            piece = landing.at[layer, first, q, j]
            for x in xs[1:]:
                send(piece, piece, relay_send, ring_sem.at[1, layer], (x, 1, j))

        def share(layer):
            await_bytes(landing.at[layer, second, 0, pl.ds(0, grid_y - 1)], ring_sem.at[0, layer])
            piece = landing.at[layer, second, q]
            send(piece, piece, relay_send, ring_sem.at[2, layer], (xs[1], 1, j))
            send(piece, piece, relay_send, ring_sem.at[3, layer], (xs[-1], 1, j))
            deliver(piece, 1, layer)
            await_bytes(landing.at[layer, first, pl.ds(0, secs - 1), 0], ring_sem.at[1, layer])
            piece = landing.at[layer, first, :, j]
            send(piece, piece, relay_send, ring_sem.at[4, layer], (q, 1, ys[1]))
            send(piece, piece, relay_send, ring_sem.at[5, layer], (q, 1, ys[-1]))
            deliver(piece, 0, layer)

        def relay(layer):
            await_bytes(landing.at[layer, second, 0], ring_sem.at[2, layer])
            piece = landing.at[layer, 2, xs[-1]]
            send(piece, piece, relay_send, ring_sem.at[6, layer], (xs[1], 1, j))
            deliver(landing.at[layer, second, xs[-1]], 1, layer)
            await_bytes(landing.at[layer, second, 0], ring_sem.at[3, layer])
            piece = landing.at[layer, 3, xs[1]]
            send(piece, piece, relay_send, ring_sem.at[7, layer], (xs[-1], 1, j))
            deliver(landing.at[layer, second, xs[1]], 1, layer)
            await_bytes(landing.at[layer, first, :, 0], ring_sem.at[4, layer])
            piece = landing.at[layer, 0, :, ys[-1]]
            send(piece, piece, relay_send, ring_sem.at[8, layer], (q, 1, ys[1]))
            deliver(landing.at[layer, first, :, ys[-1]], 0, layer)
            await_bytes(landing.at[layer, first, :, 0], ring_sem.at[5, layer])
            piece = landing.at[layer, 1, :, ys[1]]
            send(piece, piece, relay_send, ring_sem.at[9, layer], (q, 1, ys[-1]))
            deliver(landing.at[layer, first, :, ys[1]], 0, layer)

        def close_layer(layer):
            await_bytes(landing.at[layer, 2, 0], ring_sem.at[6, layer])
            await_bytes(landing.at[layer, 3, 0], ring_sem.at[7, layer])
            deliver(landing.at[layer, second, xs[2]], 1, layer)
            await_bytes(landing.at[layer, 0, :, 0], ring_sem.at[8, layer])
            await_bytes(landing.at[layer, 1, :, 0], ring_sem.at[9, layer])
            deliver(landing.at[layer, first, :, ys[2]], 0, layer)

        open_layer(0)
        open_layer(1)
        share(0)
        open_layer(2)
        share(1)
        open_layer(3)
        relay(0)
        share(2)
        relay(1)
        close_layer(0)
        share(3)
        relay(2)
        close_layer(1)
        relay(3)
        close_layer(2)
        close_layer(3)
        for layer in range(secs):
            for step in range(1, secs):
                await_bytes(landing.at[layer, second, 0, 0], relay_send)
                await_bytes(landing.at[layer, first, 0, 0], relay_send)
            for side in range(2):
                await_bytes(landing.at[layer, second, 0], relay_send)
                await_bytes(landing.at[layer, first, :, 0], relay_send)
                await_bytes(landing.at[layer, 2, 0], relay_send)
                await_bytes(landing.at[layer, 0, :, 0], relay_send)
            await_bytes(landing.at[layer], relay_send)

    @pl.when(is_consumer)
    def _():
        position = src_ref[j * secs + q]
        layer_of = position // (size * size)
        inside = position - layer_of * (size * size)
        row_of = inside // size
        column_of = inside - row_of * size
        column_ids = lax.broadcasted_iota(jnp.int32, (1, size), 1)
        on_column = jnp.where(column_ids == column_of, 1.0, 0.0).astype(f32)

        def dot(a, b):
            return jnp.dot(a, b, preferred_element_type=f32)

        def dot_turned(a, b):
            return lax.dot_general(a, b, (((1,), (1,)), ((), ())), preferred_element_type=f32)

        def front(layer, source):
            vr = source[0]
            vi = source[1]
            yr = factor[layer, 2]
            yi = factor[layer, 3]
            turned[0] = (dot_turned(vr, yr) - dot_turned(vi, yi)).astype(bf16)
            turned[1] = (dot_turned(vr, yi) + dot_turned(vi, yr)).astype(bf16)
            xr = factor[layer, 0]
            xi = factor[layer, 1]
            real = dot(xr, turned[0]) - dot(xi, turned[1])
            yield 0, real
            yield 1, dot(xr, turned[1]) + dot(xi, turned[0])

        def gather_rows(layer, planes):
            def step(k, carry):
                outer = k // grid_y
                slot = lax.rem(k, grid_y)
                for m in planes:
                    tile = jnp.concatenate(
                        [landing[layer, m, outer, i, slot] for i in range(grid_y)], axis=0
                    )
                    factor[layer, m, pl.ds(pl.multiple_of(k * 32, 32), 32), :] = tile
                return carry

            lax.fori_loop(0, size // 32, step, 0)

        def emit(layer, plane):
            def one(k, carry):
                piece = field.at[layer, plane, pl.ds(pl.multiple_of(k * rows, rows), rows), :]
                target = out_ref.at[plane, 0, :, pl.ds(pl.multiple_of(q * size, size), size)]
                here = (layer == q) & (k == p)

                @pl.when(here)
                def _():
                    pltpu.make_async_copy(piece, target, out_sem).start()

                @pl.when(jnp.logical_not(here) & (k != detour))
                def _():
                    send(piece, target, out_send, out_sem, (layer, k, j))

                @pl.when(k == detour)
                def _():
                    send(piece, hop_out.at[layer, plane], out_send, hop_out_sem.at[layer], (q, out_helper, j))

                return carry

            lax.fori_loop(0, columns, one, 0)

        half_rows = pl.ds(0, size // 2)

        def await_half(which, layer):
            await_bytes(field.at[layer, :, half_rows, :], field_sem.at[which, layer])

        def await_half_w(which, layer):
            await_bytes(weights.at[layer, half_rows, :], weight_sem.at[which, layer])

        near_chips = [*range(2, 2 + quarter), *range(columns - quarter, columns)]
        for layer in range(secs):
            await_half(0, layer)
            if layer:
                await_half_w(0, layer)
            for k in () if layer == secs - 1 else near_chips:
                pl.semaphore_signal(go_sem, inc=1, device_id=(q, k, j), device_id_type=MESH)

        def forward(layer, carry):
            await_half(1, layer)

            strength = jnp.where(layer_of == layer, source_amplitude, 0.0).astype(f32)

            def reduce_rows(k, coupled):
                part = pl.ds(pl.multiple_of(k * 32, 32), 32)
                hit = lax.broadcasted_iota(jnp.int32, (32, 1), 0) == row_of - k * 32
                bump = jnp.where(hit, strength, 0.0) * on_column
                real = field[layer, 0, part, :].astype(f32) + bump
                imag = field[layer, 1, part, :].astype(f32)
                if coupled:
                    scale = weights[layer, part, :].astype(f32)
                    real = real - scale * field[layer - 1, 0, part, :].astype(f32)
                    imag = imag - scale * field[layer - 1, 1, part, :].astype(f32)
                sent[0, part, :] = real.astype(bf16)
                sent[1, part, :] = imag.astype(bf16)

            def sweep_rows(coupled):
                def step(k, carry):
                    reduce_rows(k, coupled)
                    return carry

                lax.fori_loop(0, size // 32, step, 0, unroll=2)

            @pl.when(layer == 0)
            def _():
                sweep_rows(False)

            @pl.when(layer > 0)
            def _():
                await_half_w(1, layer)
                sweep_rows(True)

            await_bytes(landing.at[layer, pl.ds(2, 2)], plane_sem.at[1, layer])
            gather_rows(layer, (2, 3))
            await_bytes(landing.at[layer, pl.ds(0, 2)], plane_sem.at[0, layer])
            gather_rows(layer, (0, 1))
            for plane, value in front(layer, sent):
                field[layer, plane] = value.astype(bf16)

                @pl.when(layer == secs - 1)
                def _():
                    emit(layer, plane)

            return carry

        lax.fori_loop(0, secs, forward, 0)

        def backward(step, carry):
            layer = secs - 2 - step

            def couple_rows(k, carry):
                part = pl.ds(pl.multiple_of(k * 32, 32), 32)
                scale = weights[layer + 1, part, :].astype(f32)
                for m in range(2):
                    sent[m, part, :] = (scale * field[layer + 1, m, part, :].astype(f32)).astype(bf16)
                return carry

            lax.fori_loop(0, size // 32, couple_rows, 0, unroll=2)
            for plane, value in front(layer, sent):
                solved = value.astype(bf16).astype(f32)
                field[layer, plane] = (field[layer, plane].astype(f32) - solved).astype(bf16)
                emit(layer, plane)
            return carry

        lax.fori_loop(0, secs - 1, backward, 0)
        await_bytes(field.at[pl.ds(0, secs - 1)], out_send)
        await_bytes(field.at[0, :, pl.ds(0, size - rows), :], out_send)

    @pl.when(p == out_helper)
    def _():
        for layer in range(secs - 1, -1, -1):
            await_bytes(hop_out.at[layer], hop_out_sem.at[layer])
            send(hop_out.at[layer], source_block_of(out_ref, q), hop_send, out_sem, (layer, detour, j))
        await_bytes(hop_out, hop_send)

    @pl.when(jnp.logical_not(is_own_hub))
    def _():
        await_bytes(landing.at[0, :, 0, 0, 0], block_send)

    await_bytes(stage.at[pl.ds(0, secs - 1)], swap_send)

    @pl.when(q > 0)
    def _():
        await_bytes(stage_w.at[pl.ds(0, secs - 1)], swap_send)

    @pl.when(jnp.logical_not(is_near))
    def _():
        for layer in range(secs - 2, secs):
            await_sent(layer)

    @pl.when(is_near)
    def _():
        for layer in range(secs - 1, secs):
            await_sent(layer)


    @pl.when(p == helper)
    def _():
        await_bytes(hop, hop_send)
        await_bytes(hop_w.at[pl.ds(0, secs - 1)], hop_send)

    await_bytes(out_ref, out_sem)


def solution(mesh):
    secs = mesh.shape["sec"]
    columns = mesh.shape["px"]
    grid_y = mesh.shape["py"]

    def on_device(background, src_pos, coupling, x_factor, y_factor):
        size = x_factor.shape[3]
        height = x_factor.shape[2]
        dims = (secs, columns, grid_y, size)

        def body(*refs):
            sweep_kernel(dims, *refs)

        any_spec = pl.BlockSpec(memory_space=pl.ANY)
        dma = pltpu.SemaphoreType.DMA
        return pl.pallas_call(
            body,
            out_shape=jax.ShapeDtypeStruct(background.shape, bf16),
            in_specs=[pl.BlockSpec(memory_space=pltpu.SMEM)] + [any_spec] * 4,
            out_specs=any_spec,
            scratch_shapes=[
                pltpu.VMEM((secs, 4, columns // grid_y, grid_y, grid_y, height, size), bf16),
                pltpu.VMEM((secs, 2, size // columns, size), bf16),
                pltpu.VMEM((secs, size // columns, size), bf16),
                pltpu.VMEM((secs, 4, size, size), bf16),
                pltpu.VMEM((secs, 2, size, size), bf16),
                pltpu.VMEM((secs, size, size), bf16),
                pltpu.VMEM((2, size, size), bf16),
                pltpu.VMEM((2, size, size), bf16),
                dma, dma, dma((secs,)), dma, dma,
                dma((secs,)), dma((secs,)), dma((secs,)), dma((10, secs)), dma((2, secs)),
                dma((2, secs)), dma((2, secs)), dma,
                pltpu.VMEM((secs, 2, size // columns, size), bf16),
                pltpu.VMEM((secs, size // columns, size), bf16),
                pltpu.VMEM((secs, 2, size // columns, size), bf16),
                dma, dma((secs,)), dma((secs,)), dma((secs,)), pltpu.SemaphoreType.REGULAR,
            ],
            compiler_params=pltpu.CompilerParams(
                collective_id=0, has_side_effects=True, vmem_limit_bytes=60 * 2**20
            ),
            name="sweep",
        )(src_pos, background, coupling, x_factor, y_factor)

    placed = (
        P(None, "sec", "px", "py"),
        P(),
        P("sec", "px", None),
        P("sec", None, ("px", "py"), None),
        P("sec", None, ("px", "py"), None),
    )
    return jax.shard_map(
        on_device, mesh=mesh, in_specs=placed, out_specs=P(None, "sec", "px", "py"), check_vma=False
    )
```

```python
import jax
import jax.numpy as jnp
from jax import lax
from jax.experimental import pallas as pl
from jax.experimental.pallas import tpu as pltpu
from jax.sharding import PartitionSpec as P

MESH = pl.DeviceIdType.MESH
source_amplitude = 8.0
f32 = jnp.float32
bf16 = jnp.bfloat16


def sweep_kernel(
    dims, src_ref, bg_ref, cp_ref, xf_ref, yf_ref, out_ref,
    landing, stage, stage_w, factor, field, weights, sent, turned,
    block_send, swap_send, field_send, relay_send, out_send,
    block_sem, swap_sem, swap_w_sem, ring_sem, plane_sem, field_sem, weight_sem, out_sem,
    hop, hop_w, hop_out, hop_send, hop_sem, hop_w_sem, hop_out_sem, go_sem,
):
    secs, columns, grid_y, size = dims
    rows = size // columns
    q = lax.axis_index("sec")
    p = lax.axis_index("px")
    j = lax.axis_index("py")
    group = p // grid_y
    inner = lax.rem(p, grid_y)
    is_consumer = p == 0
    is_relay = p == 1
    hub = (group, 1, j)
    quarter = columns // 4
    is_near = ((p >= 2) & (p < 2 + quarter)) | (p >= columns - quarter)
    detour = columns // 2 + 1
    helper = columns // 2 - 1
    out_helper = columns // 2 + 3
    is_own_hub = is_relay & (q == group)

    barrier = pltpu.get_barrier_semaphore()

    def greet(device):
        pl.semaphore_signal(barrier, inc=1, device_id=device, device_id_type=MESH)

    @pl.when(is_relay)
    def _():
        for a in (2, 1, 3, 0):
            for b in range(grid_y):
                greet((lax.rem(q + a, secs), q * grid_y + b, j))
        for step in range(1, secs):
            greet((lax.rem(q + step, secs), 1, j))
        for step in range(1, grid_y):
            greet((q, 1, lax.rem(j + step, grid_y)))

    @pl.when(is_consumer)
    def _():
        for b in range(columns):
            greet((q, (b + columns // 4) % columns, j))

    for step in range(1, secs):
        greet((lax.rem(q + step, secs), p, j))

    for a in range(secs):
        greet((a, 0, j))

    @pl.when(p == helper)
    def _():
        greet((q, detour, j))

    @pl.when(p == detour)
    def _():
        for a in range(secs):
            greet((a, out_helper, j))

    expected = secs + 1 + jnp.where(is_consumer, secs * columns, 0)
    expected = expected + jnp.where(is_relay, secs + grid_y - 2, 0)
    expected = expected + jnp.where(p == detour, 1, 0)
    expected = expected + jnp.where(p == out_helper, secs, 0)
    pl.semaphore_wait(barrier, expected)

    def await_bytes(ref, sem):
        pltpu.make_async_copy(ref, ref, sem).wait()

    def send(src, dst, send_sem, recv_sem, device):
        pltpu.make_async_remote_copy(
            src_ref=src, dst_ref=dst, send_sem=send_sem, recv_sem=recv_sem,
            device_id=device, device_id_type=MESH,
        ).start()

    def push(src, dst, send_sem, recv_sem, device, is_self):
        @pl.when(is_self)
        def _():
            pltpu.make_async_copy(src, dst, recv_sem).start()

        @pl.when(jnp.logical_not(is_self))
        def _():
            send(src, dst, send_sem, recv_sem, device)

    push(
        yf_ref.at[0], landing.at[q, pl.ds(2, 2), group, j, inner], block_send, block_sem.at[q],
        hub, is_own_hub,
    )
    push(
        xf_ref.at[0], landing.at[q, pl.ds(0, 2), group, j, inner], block_send, block_sem.at[q],
        hub, is_own_hub,
    )

    def source_block_of(ref, a):
        return ref.at[:, 0, :, pl.ds(pl.multiple_of(a * size, size), size)]

    def source_block(a):
        return source_block_of(bg_ref, a)

    for step in range(1, secs):
        a = lax.rem(q + step, secs)
        send(source_block(a), stage.at[q], swap_send, swap_sem.at[q], (a, p, j))

    @pl.when(q > 0)
    def _():
        for step in range(1, secs):
            a = lax.rem(q + step, secs)
            send(cp_ref.at[0], stage_w.at[q], swap_send, swap_w_sem.at[q], (a, p, j))

    for layer in range(secs):

        @pl.when(q != layer)
        def _():
            await_bytes(stage.at[layer], swap_sem.at[layer])

    home = (q, 0, j)
    half = jnp.where(is_near, 1, 0)

    def rows_of(k):
        return pl.ds(pl.multiple_of(k * rows, rows), rows)

    def pass_on(layer, block, block_w):
        @pl.when(p == detour)
        def _():
            send(block, hop.at[layer], field_send.at[layer], hop_sem.at[layer], (q, helper, j))

        @pl.when(p != detour)
        def _():
            push(
                block, field.at[layer, :, rows_of(p), :], field_send.at[layer], field_sem.at[half, layer],
                home, is_consumer,
            )

        if layer:

            @pl.when(q != layer)
            def _():
                await_bytes(stage_w.at[layer], swap_w_sem.at[layer])

            @pl.when(p == detour)
            def _():
                send(block_w, hop_w.at[layer], field_send.at[layer], hop_w_sem.at[layer], (q, helper, j))

            @pl.when(p != detour)
            def _():
                push(
                    block_w, weights.at[layer, rows_of(p), :], field_send.at[layer],
                    weight_sem.at[half, layer], home, is_consumer,
                )

    def await_sent(layer):
        @pl.when(jnp.logical_not(is_consumer))
        def _():
            await_bytes(stage.at[layer], field_send.at[layer])
            if layer:
                await_bytes(stage_w.at[layer], field_send.at[layer])

    for layer in range(secs):

        if layer:

            @pl.when(is_near)
            def _():
                pl.semaphore_wait(go_sem, 1)

        if layer >= 2:

            @pl.when(jnp.logical_not(is_near))
            def _():
                await_sent(layer - 2)

        if layer >= 1:

            @pl.when(is_near)
            def _():
                await_sent(layer - 1)


        @pl.when(q == layer)
        def _():
            pass_on(layer, source_block(q), cp_ref.at[0])

        @pl.when(q != layer)
        def _():
            pass_on(layer, stage.at[layer], stage_w.at[layer])

    @pl.when(p == helper)
    def _():
        for layer in range(secs):
            await_bytes(hop.at[layer], hop_sem.at[layer])
            send(
                hop.at[layer], field.at[layer, :, pl.ds(detour * rows, rows), :], hop_send,
                field_sem.at[0, layer], home,
            )
            if layer:
                await_bytes(hop_w.at[layer], hop_w_sem.at[layer])
                send(
                    hop_w.at[layer], weights.at[layer, pl.ds(detour * rows, rows), :], hop_send,
                    weight_sem.at[0, layer], home,
                )

    @pl.when(is_relay)
    def _():
        xs = [lax.rem(q + step, secs) for step in range(secs)]
        ys = [lax.rem(j + step, grid_y) for step in range(grid_y)]
        first = pl.ds(0, 2)
        second = pl.ds(2, 2)

        def deliver(piece, part, layer):
            send(piece, piece, relay_send, plane_sem.at[part, layer], home)

        def open_layer(layer):
            await_bytes(landing.at[layer, :, 0, 0], block_sem.at[layer])
            piece = landing.at[layer, second, q, j]
            for y in ys[1:]:
                send(piece, piece, relay_send, ring_sem.at[0, layer], (q, 1, y))
            piece = landing.at[layer, first, q, j]
            for x in xs[1:]:
                send(piece, piece, relay_send, ring_sem.at[1, layer], (x, 1, j))

        def share(layer):
            await_bytes(landing.at[layer, second, 0, pl.ds(0, grid_y - 1)], ring_sem.at[0, layer])
            piece = landing.at[layer, second, q]
            send(piece, piece, relay_send, ring_sem.at[2, layer], (xs[1], 1, j))
            send(piece, piece, relay_send, ring_sem.at[3, layer], (xs[-1], 1, j))
            deliver(piece, 1, layer)
            await_bytes(landing.at[layer, first, pl.ds(0, secs - 1), 0], ring_sem.at[1, layer])
            piece = landing.at[layer, first, :, j]
            send(piece, piece, relay_send, ring_sem.at[4, layer], (q, 1, ys[1]))
            send(piece, piece, relay_send, ring_sem.at[5, layer], (q, 1, ys[-1]))
            deliver(piece, 0, layer)

        def relay(layer):
            await_bytes(landing.at[layer, second, 0], ring_sem.at[2, layer])
            piece = landing.at[layer, 2, xs[-1]]
            send(piece, piece, relay_send, ring_sem.at[6, layer], (xs[1], 1, j))
            deliver(landing.at[layer, second, xs[-1]], 1, layer)
            await_bytes(landing.at[layer, second, 0], ring_sem.at[3, layer])
            piece = landing.at[layer, 3, xs[1]]
            send(piece, piece, relay_send, ring_sem.at[7, layer], (xs[-1], 1, j))
            deliver(landing.at[layer, second, xs[1]], 1, layer)
            await_bytes(landing.at[layer, first, :, 0], ring_sem.at[4, layer])
            piece = landing.at[layer, 0, :, ys[-1]]
            send(piece, piece, relay_send, ring_sem.at[8, layer], (q, 1, ys[1]))
            deliver(landing.at[layer, first, :, ys[-1]], 0, layer)
            await_bytes(landing.at[layer, first, :, 0], ring_sem.at[5, layer])
            piece = landing.at[layer, 1, :, ys[1]]
            send(piece, piece, relay_send, ring_sem.at[9, layer], (q, 1, ys[-1]))
            deliver(landing.at[layer, first, :, ys[1]], 0, layer)

        def close_layer(layer):
            await_bytes(landing.at[layer, 2, 0], ring_sem.at[6, layer])
            await_bytes(landing.at[layer, 3, 0], ring_sem.at[7, layer])
            deliver(landing.at[layer, second, xs[2]], 1, layer)
            await_bytes(landing.at[layer, 0, :, 0], ring_sem.at[8, layer])
            await_bytes(landing.at[layer, 1, :, 0], ring_sem.at[9, layer])
            deliver(landing.at[layer, first, :, ys[2]], 0, layer)

        open_layer(0)
        open_layer(1)
        share(0)
        open_layer(2)
        share(1)
        open_layer(3)
        relay(0)
        share(2)
        relay(1)
        close_layer(0)
        share(3)
        relay(2)
        close_layer(1)
        relay(3)
        close_layer(2)
        close_layer(3)
        for layer in range(secs):
            for step in range(1, secs):
                await_bytes(landing.at[layer, second, 0, 0], relay_send)
                await_bytes(landing.at[layer, first, 0, 0], relay_send)
            for side in range(2):
                await_bytes(landing.at[layer, second, 0], relay_send)
                await_bytes(landing.at[layer, first, :, 0], relay_send)
                await_bytes(landing.at[layer, 2, 0], relay_send)
                await_bytes(landing.at[layer, 0, :, 0], relay_send)
            await_bytes(landing.at[layer], relay_send)

    @pl.when(is_consumer)
    def _():
        position = src_ref[j * secs + q]
        layer_of = position // (size * size)
        inside = position - layer_of * (size * size)
        row_of = inside // size
        column_of = inside - row_of * size
        column_ids = lax.broadcasted_iota(jnp.int32, (1, size), 1)
        on_column = jnp.where(column_ids == column_of, 1.0, 0.0).astype(f32)

        def dot(a, b):
            return jnp.dot(a, b, preferred_element_type=f32)

        def dot_turned(a, b):
            return lax.dot_general(a, b, (((1,), (1,)), ((), ())), preferred_element_type=f32)

        def front(layer, source):
            vr = source[0]
            vi = source[1]
            yr = factor[layer, 2]
            yi = factor[layer, 3]
            turned[0] = (dot_turned(vr, yr) - dot_turned(vi, yi)).astype(bf16)
            turned[1] = (dot_turned(vr, yi) + dot_turned(vi, yr)).astype(bf16)
            xr = factor[layer, 0]
            xi = factor[layer, 1]
            real = dot(xr, turned[0]) - dot(xi, turned[1])
            yield 0, real
            yield 1, dot(xr, turned[1]) + dot(xi, turned[0])

        def gather_rows(layer, planes):
            def step(k, carry):
                outer = k // grid_y
                slot = lax.rem(k, grid_y)
                for m in planes:
                    tile = jnp.concatenate(
                        [landing[layer, m, outer, i, slot] for i in range(grid_y)], axis=0
                    )
                    factor[layer, m, pl.ds(pl.multiple_of(k * 32, 32), 32), :] = tile
                return carry

            lax.fori_loop(0, size // 32, step, 0)

        def emit(layer, plane):
            target = out_ref.at[plane, 0, :, pl.ds(pl.multiple_of(q * size, size), size)]
            for k in range(columns):
                piece = field.at[layer, plane, pl.ds(k * rows, rows), :]
                if k == 0:
                    push(piece, target, out_send, out_sem, (layer, k, j), layer == q)
                elif k == detour:
                    send(piece, hop_out.at[layer, plane], out_send, hop_out_sem.at[layer], (q, out_helper, j))
                else:
                    send(piece, target, out_send, out_sem, (layer, k, j))

        half_rows = pl.ds(0, size // 2)

        def await_half(which, layer):
            await_bytes(field.at[layer, :, half_rows, :], field_sem.at[which, layer])

        def await_half_w(which, layer):
            await_bytes(weights.at[layer, half_rows, :], weight_sem.at[which, layer])

        near_chips = [*range(2, 2 + quarter), *range(columns - quarter, columns)]
        for layer in range(3):
            await_half(0, layer)
            if layer:
                await_half_w(0, layer)
            waves = 0 if layer == secs - 1 else 1
            for k in near_chips if waves else ():
                pl.semaphore_signal(go_sem, inc=waves, device_id=(q, k, j), device_id_type=MESH)

        def forward(layer, carry):
            await_half(1, layer)

            @pl.when(layer >= 3)
            def _():
                await_half(0, layer)
                await_half_w(0, layer)


            strength = jnp.where(layer_of == layer, source_amplitude, 0.0).astype(f32)

            def reduce_rows(k, coupled):
                part = pl.ds(pl.multiple_of(k * 32, 32), 32)
                hit = lax.broadcasted_iota(jnp.int32, (32, 1), 0) == row_of - k * 32
                bump = jnp.where(hit, strength, 0.0) * on_column
                real = field[layer, 0, part, :].astype(f32) + bump
                imag = field[layer, 1, part, :].astype(f32)
                if coupled:
                    scale = weights[layer, part, :].astype(f32)
                    real = real - scale * field[layer - 1, 0, part, :].astype(f32)
                    imag = imag - scale * field[layer - 1, 1, part, :].astype(f32)
                sent[0, part, :] = real.astype(bf16)
                sent[1, part, :] = imag.astype(bf16)

            def sweep_rows(coupled):
                def step(k, carry):
                    reduce_rows(k, coupled)
                    return carry

                lax.fori_loop(0, size // 32, step, 0, unroll=2)

            @pl.when(layer == 0)
            def _():
                sweep_rows(False)

            @pl.when(layer > 0)
            def _():
                await_half_w(1, layer)
                sweep_rows(True)

            await_bytes(landing.at[layer, pl.ds(2, 2)], plane_sem.at[1, layer])
            gather_rows(layer, (2, 3))
            await_bytes(landing.at[layer, pl.ds(0, 2)], plane_sem.at[0, layer])
            gather_rows(layer, (0, 1))
            for plane, value in front(layer, sent):
                field[layer, plane] = value.astype(bf16)

                @pl.when(layer == secs - 1)
                def _():
                    emit(layer, plane)

            return carry

        lax.fori_loop(0, secs, forward, 0)

        def backward(step, carry):
            layer = secs - 2 - step

            def couple_rows(k, carry):
                part = pl.ds(pl.multiple_of(k * 32, 32), 32)
                scale = weights[layer + 1, part, :].astype(f32)
                for m in range(2):
                    sent[m, part, :] = (scale * field[layer + 1, m, part, :].astype(f32)).astype(bf16)
                return carry

            lax.fori_loop(0, size // 32, couple_rows, 0, unroll=2)
            for plane, value in front(layer, sent):
                solved = value.astype(bf16).astype(f32)
                field[layer, plane] = (field[layer, plane].astype(f32) - solved).astype(bf16)
                emit(layer, plane)
            return carry

        lax.fori_loop(0, secs - 1, backward, 0)
        await_bytes(field.at[pl.ds(0, secs - 1)], out_send)
        await_bytes(field.at[0, :, pl.ds(0, size - rows), :], out_send)

    @pl.when(p == out_helper)
    def _():
        for layer in range(secs - 1, -1, -1):
            await_bytes(hop_out.at[layer], hop_out_sem.at[layer])
            send(hop_out.at[layer], source_block_of(out_ref, q), hop_send, out_sem, (layer, detour, j))
        await_bytes(hop_out, hop_send)

    @pl.when(jnp.logical_not(is_own_hub))
    def _():
        await_bytes(landing.at[0, :, 0, 0, 0], block_send)

    await_bytes(stage.at[pl.ds(0, secs - 1)], swap_send)

    @pl.when(q > 0)
    def _():
        await_bytes(stage_w.at[pl.ds(0, secs - 1)], swap_send)

    @pl.when(jnp.logical_not(is_near))
    def _():
        for layer in range(secs - 2, secs):
            await_sent(layer)

    @pl.when(is_near)
    def _():
        for layer in range(secs - 1, secs):
            await_sent(layer)


    @pl.when(p == helper)
    def _():
        await_bytes(hop, hop_send)
        await_bytes(hop_w.at[pl.ds(0, secs - 1)], hop_send)

    await_bytes(out_ref, out_sem)


def solution(mesh):
    secs = mesh.shape["sec"]
    columns = mesh.shape["px"]
    grid_y = mesh.shape["py"]

    def on_device(background, src_pos, coupling, x_factor, y_factor):
        size = x_factor.shape[3]
        height = x_factor.shape[2]
        dims = (secs, columns, grid_y, size)

        def body(*refs):
            sweep_kernel(dims, *refs)

        any_spec = pl.BlockSpec(memory_space=pl.ANY)
        dma = pltpu.SemaphoreType.DMA
        return pl.pallas_call(
            body,
            out_shape=jax.ShapeDtypeStruct(background.shape, bf16),
            in_specs=[pl.BlockSpec(memory_space=pltpu.SMEM)] + [any_spec] * 4,
            out_specs=any_spec,
            scratch_shapes=[
                pltpu.VMEM((secs, 4, columns // grid_y, grid_y, grid_y, height, size), bf16),
                pltpu.VMEM((secs, 2, size // columns, size), bf16),
                pltpu.VMEM((secs, size // columns, size), bf16),
                pltpu.VMEM((secs, 4, size, size), bf16),
                pltpu.VMEM((secs, 2, size, size), bf16),
                pltpu.VMEM((secs, size, size), bf16),
                pltpu.VMEM((2, size, size), bf16),
                pltpu.VMEM((2, size, size), bf16),
                dma, dma, dma((secs,)), dma, dma,
                dma((secs,)), dma((secs,)), dma((secs,)), dma((10, secs)), dma((2, secs)),
                dma((2, secs)), dma((2, secs)), dma,
                pltpu.VMEM((secs, 2, size // columns, size), bf16),
                pltpu.VMEM((secs, size // columns, size), bf16),
                pltpu.VMEM((secs, 2, size // columns, size), bf16),
                dma, dma((secs,)), dma((secs,)), dma((secs,)), pltpu.SemaphoreType.REGULAR,
            ],
            compiler_params=pltpu.CompilerParams(
                collective_id=0, has_side_effects=True, vmem_limit_bytes=60 * 2**20
            ),
            name="sweep",
        )(src_pos, background, coupling, x_factor, y_factor)

    placed = (
        P(None, "sec", "px", "py"),
        P(),
        P("sec", "px", None),
        P("sec", None, ("px", "py"), None),
        P("sec", None, ("px", "py"), None),
    )
    return jax.shard_map(
        on_device, mesh=mesh, in_specs=placed, out_specs=P(None, "sec", "px", "py"), check_vma=False
    )
```
